256 devices in a mesh: pair: 64 (over y, z, core), row: 4 (over x).
Axes of the slice: x: 4, y: 4, z: 8, core: 2. Of those that a mesh axis runs over, the one named last changes fastest.
Arguments:
- whitened: float32 [4096, 16384], P('row', 'pair'), may hold values from -50 to 50, as said below
- offsets: int32 [4, 4], replicated, may hold values from 0 to 127
Outputs:
- rotated: float32 [4096, 16384], P('row', 'pair')
- right_vectors: float32 [16384, 16384], P('row', 'pair')
The draws below stay inside these ranges and needn't reach their ends.
Inputs may be any that keep to these rules, and one draw needn't show every extreme that they name: whitened has rows and columns of different scales.
All inputs are finite; a program needn't handle non-finite values.
Results may differ from the reference program's by a relative error of at most 0.0003.
Values sent between devices are 32-bit elements; how exact they have to be, the bound alone decides.
A program may use at most 64 MiB of HBM per device.

```python
import math
import jax
import jax.numpy as jnp
from jax import lax

B = 128
ROUNDS = 4
STEPS = 4
ROWS = 4096
COLS = 16384
N_PAIR = 64


def draw_whitened(key, part):
    keys = jax.random.split(key, 3)
    position = jnp.arange(ROWS, dtype=jnp.float32)
    ramp = 0.5 + position / ROWS
    row_scale = jnp.exp(jax.random.uniform(keys[1], (ROWS,), jnp.float32, math.log(0.3), math.log(3.0))) * ramp
    col_scale = jnp.exp(jax.random.uniform(keys[2], (COLS,), jnp.float32, math.log(0.5), math.log(2.0)))
    base = jnp.clip(jax.random.normal(keys[0], (ROWS, COLS), jnp.float32), -4.0, 4.0)
    return (base * row_scale[:, None] * col_scale[None, :]).astype(jnp.float32)


def plant(entries, rng, smallest, high):
    place = [jax.random.randint(jax.random.fold_in(rng, axis), (), 0, length) for axis, length in enumerate(entries.shape)]
    main_axis = entries.shape.index(max(entries.shape))
    beside = place[:main_axis] + [(place[main_axis] + 1) % entries.shape[main_axis]] + place[main_axis + 1:]
    return entries.at[tuple(place)].set(smallest).at[tuple(beside)].set(high)


def setup_inputs(seed: int = 0) -> dict:
    seeds = jax.random.split(jax.random.key(seed), 3)
    return {
        "whitened": draw_whitened(jax.random.fold_in(seeds[2], 71), 0),
        "offsets": plant(jax.random.randint(seeds[1], (STEPS, ROUNDS), 0, B), jax.random.fold_in(seeds[1], 1), 0, B - 1).astype(jnp.int32),
    }


def pair_rounds(pair_gram, step_offsets):
    full_width = pair_gram.shape[0]
    half_width = full_width // 2
    position = jnp.arange(half_width, dtype=jnp.int32)
    accumulated = jnp.eye(full_width, dtype=pair_gram.dtype)
    for round_index in range(ROUNDS):
        shift_by = step_offsets[round_index]
        permute = (position[None, :] == (position[:, None] + shift_by) % half_width).astype(pair_gram.dtype)
        diagonal = jnp.diagonal(pair_gram)
        first_diag = diagonal[:half_width]
        second = lax.optimization_barrier(jnp.sum(permute * diagonal[half_width:][None, :], axis=1))
        across = lax.optimization_barrier(jnp.sum(pair_gram[:half_width, half_width:] * permute, axis=1))
        half_gap = 0.5 * (second - first_diag)
        radius = jnp.sqrt(half_gap * half_gap + across * across)
        direction = jnp.where(half_gap >= 0, 1.0, -1.0).astype(pair_gram.dtype)
        tangent = -direction * across / (jnp.abs(half_gap) + radius + 1e-06 * (first_diag + second))
        cosine = 1.0 / jnp.sqrt(1.0 + tangent * tangent)
        sine_part = tangent * cosine
        moved_sine = sine_part[:, None] * permute
        cos_second = lax.optimization_barrier(jnp.sum(permute * cosine[:, None], axis=0))
        upper_rows = jnp.concatenate([jnp.diag(cosine), -moved_sine], axis=1)
        lower_rows = jnp.concatenate([moved_sine.T, jnp.diag(cos_second)], axis=1)
        rotation = jnp.concatenate([upper_rows, lower_rows], axis=0)
        pair_gram = jnp.dot(rotation.T, jnp.dot(pair_gram, rotation, precision=lax.Precision.HIGHEST), precision=lax.Precision.HIGHEST)
        accumulated = jnp.dot(accumulated, rotation, precision=lax.Precision.HIGHEST)
    return (pair_gram, accumulated)

def advance(stacked):
    tops = stacked[:, :, :B]
    bottoms = stacked[:, :, B:]
    new_tops = jnp.concatenate([tops[:1], bottoms[:1], tops[1:-1]], axis=0)
    new_bottoms = jnp.concatenate([bottoms[1:], tops[-1:]], axis=0)
    return jnp.concatenate([new_tops, new_bottoms], axis=2)

def reference(whitened, offsets):
    row_count = whitened.shape[0]
    col_count = whitened.shape[1]
    blocks = whitened.reshape(row_count, N_PAIR, 2 * B).transpose(1, 0, 2)
    vectors = jnp.eye(col_count, dtype=whitened.dtype).reshape(col_count, N_PAIR, 2 * B).transpose(1, 0, 2)
    for step_index in range(STEPS):
        grams = jnp.einsum('pmi,pmj->pij', blocks, blocks, precision=lax.Precision.HIGHEST)
        step_offsets = offsets[step_index]

        def solve_one(single):
            return pair_rounds(single, step_offsets)[1]
        rotations = jax.vmap(solve_one)(grams)
        blocks = jnp.einsum('pmi,pij->pmj', blocks, rotations, precision=lax.Precision.HIGHEST)
        vectors = jnp.einsum('pmi,pij->pmj', vectors, rotations, precision=lax.Precision.HIGHEST)
        if step_index + 1 < STEPS:
            blocks = advance(blocks)
            vectors = advance(vectors)
    rotated = blocks.transpose(1, 0, 2).reshape(row_count, col_count)
    right_vectors = vectors.transpose(1, 0, 2).reshape(col_count, col_count)
    return (rotated, right_vectors)
```

```python
import functools

import jax
import jax.numpy as jnp
from jax import lax
from jax.experimental import pallas as pl
from jax.experimental.pallas import tpu as pltpu
from jax.sharding import PartitionSpec as P

B = 128
ROUNDS = 4
STEPS = 4
CHUNKS = 4
MESH = pl.DeviceIdType.MESH
F32 = jnp.float32


def cross(left, right):
    return lax.dot_general(
        left, right, (((0,), (0,)), ((), ())), precision=lax.Precision.HIGHEST, preferred_element_type=F32
    )


def turns(offs_ref, step):
    offs = [offs_ref[step, r] for r in range(ROUNDS)]
    before = [jnp.int32(0)] + offs[:-1]
    return [lax.rem(b - o + B, B) for b, o in zip(before, offs)], offs[-1]


def rolled(x, shift):
    return pltpu.roll(x, shift, 1)


def jacobi(gram_a, gram_b, gram_d, shifts, back, cs_ref):
    eye = lax.broadcasted_iota(jnp.int32, (B, B), 0) == lax.broadcasted_iota(jnp.int32, (B, B), 1)

    def diag(m):
        return jnp.sum(jnp.where(eye, m, 0.0), axis=0, keepdims=True)

    for r in range(ROUNDS):
        gram_b = rolled(gram_b, shifts[r])
        gram_d = rolled(rolled(gram_d, shifts[r]).T, shifts[r])
        gram_e = gram_b.T
        a, d, c0 = diag(gram_a), diag(gram_d), diag(gram_b)
        gap = 0.5 * (d - a)
        radius = jnp.sqrt(gap * gap + c0 * c0)
        sign = jnp.where(gap >= 0, 1.0, -1.0)
        t = -sign * c0 / (jnp.abs(gap) + radius + 1e-06 * (a + d))
        c = 1.0 / jnp.sqrt(1.0 + t * t)
        s = t * c
        cs_ref[pl.ds(r, 1), :] = c
        cs_ref[pl.ds(ROUNDS + r, 1), :] = s
        col_c = jnp.broadcast_to(c, (B, B)).T
        col_s = jnp.broadcast_to(s, (B, B)).T
        y11 = gram_a * c + gram_b * s
        y12 = gram_b * c - gram_a * s
        y21 = gram_e * c + gram_d * s
        y22 = gram_d * c - gram_e * s
        gram_a = col_c * y11 + col_s * y21
        gram_b = col_c * y12 + col_s * y22
        gram_d = col_c * y22 - col_s * y12
    gram_d = rolled(rolled(gram_d, back).T, back)
    return gram_a, gram_d


def rotated(f, s, cs_ref, shifts, back):
    for r in range(ROUNDS):
        s = rolled(s, shifts[r])
        c = cs_ref[pl.ds(r, 1), :]
        n = cs_ref[pl.ds(ROUNDS + r, 1), :]
        f, s = f * c + s * n, s * c - f * n
    return f, rolled(s, back)


def rotate_rows(src_f, src_s, dst_f, dst_s, start, count, cs_ref, shifts, back, tile=64):
    def one(i, carry):
        at = pl.ds(pl.multiple_of(start + i * tile, 8), tile)
        f, s = rotated(src_f[at, :], src_s[at, :], cs_ref, shifts, back)
        dst_f[at, :] = f
        dst_s[at, :] = s
        return carry

    lax.fori_loop(0, count // tile, one, 0)


def main_kernel(
    n_pair, n_row, rows, offs_ref, x_ref, x3f, x3s, w3f, w3s, cs_out,
    xf, xs, of, os_, wf1, ws1, wf2, ws2, wof0, wos0, wof1, wos1, wof2, wos2,
    g0, gs, ad_out, ad_in, cs,
    g_send, g_recv, x_send, x_recv, ad_send, ad_recv, w_send, w_recv,
):
    k = lax.axis_index("pair")
    me = lax.axis_index("row")
    first, last = k == 0, k == n_pair - 1
    chunk = rows // CHUNKS
    width = 2 * B
    wf, ws = [None, wf1, wf2, w3f], [None, ws1, ws2, w3s]
    wof, wos = [wof0, wof1, wof2], [wos0, wos1, wos2]

    def in_f(step):
        return x3f if step == STEPS - 1 else xf.at[step]

    def in_s(step):
        return x3s if step == STEPS - 1 else xs.at[step]

    barrier = pltpu.get_barrier_semaphore()

    @pl.when(k > 0)
    def _():
        pl.semaphore_signal(barrier, inc=1, device_id={"pair": k - 1}, device_id_type=MESH)

    @pl.when(k < n_pair - 1)
    def _():
        pl.semaphore_signal(barrier, inc=1, device_id={"pair": k + 1}, device_id_type=MESH)

    for j in range(1, n_row):
        pl.semaphore_signal(barrier, inc=1, device_id={"row": lax.rem(me + j, n_row)}, device_id_type=MESH)

    def to_right(src, dst, sems, at):
        return pltpu.make_async_remote_copy(
            src_ref=src, dst_ref=dst, send_sem=sems[0].at[(0,) + at], recv_sem=sems[1].at[(0,) + at],
            device_id={"pair": k + 1}, device_id_type=MESH,
        )

    def to_left(src, dst, sems, at):
        return pltpu.make_async_remote_copy(
            src_ref=src, dst_ref=dst, send_sem=sems[0].at[(1,) + at], recv_sem=sems[1].at[(1,) + at],
            device_id={"pair": k - 1}, device_id_type=MESH,
        )

    def pass_on(f, s, dst_f, dst_s, sems, at, keep_f, keep_s):
        @pl.when(first)
        def _():
            to_right(s, dst_f, sems, at).start()
            keep_f()

        @pl.when(jnp.logical_and(k > 0, k < n_pair - 1))
        def _():
            to_right(f, dst_f, sems, at).start()

        @pl.when(last)
        def _():
            keep_s()

        @pl.when(k > 0)
        def _():
            to_left(s, dst_s, sems, at).start()

    def arrived(dst_f, dst_s, sems, at):
        @pl.when(k > 0)
        def _():
            to_right(dst_f, dst_f, sems, at).wait_recv()

        @pl.when(k < n_pair - 1)
        def _():
            to_left(dst_s, dst_s, sems, at).wait_recv()

    def sent(f, s, sems, at):
        @pl.when(k < n_pair - 1)
        def _():
            to_right(f, f, sems, at).wait_send()

        @pl.when(k > 0)
        def _():
            to_left(s, s, sems, at).wait_send()

    def peer_copy(buf, step, slot, to):
        return pltpu.make_async_remote_copy(
            src_ref=buf.at[slot], dst_ref=buf.at[slot], send_sem=g_send.at[step, to],
            recv_sem=g_recv.at[step, slot], device_id={"row": to}, device_id_type=MESH,
        )

    x_sems, ad_sems, w_sems = (x_send, x_recv), (ad_send, ad_recv), (w_send, w_recv)

    def move_w(step):
        shifts, back = turns(offs_ref, step)
        size = width * (step + 1)
        if step == 0:
            row = lax.broadcasted_iota(jnp.int32, (width, B), 0)
            col = lax.broadcasted_iota(jnp.int32, (width, B), 1)
            wof[0][...] = jnp.where(row == col, 1.0, 0.0).astype(F32)
            wos[0][...] = jnp.where(row == col + B, 1.0, 0.0).astype(F32)
            rotate_rows(wof[0], wos[0], wof[0], wos[0], 0, size, cs.at[step], shifts, back)
        else:
            arrived(wf[step].at[pl.ds(0, width * step)], ws[step].at[pl.ds(width, width * step)], w_sems, (step,))
            rotate_rows(wf[step], ws[step], wof[step], wos[step], 0, size, cs.at[step], shifts, back)
        nf, ns = wf[step + 1], ws[step + 1]

        def keep_f():
            for i in range(step + 1):
                nf[pl.ds((step - i) * width, width), :] = wof[step][pl.ds(i * width, width), :]

        def keep_s():
            for i in range(step + 1):
                ns[pl.ds((step - i + 1) * width, width), :] = wof[step][pl.ds(i * width, width), :]

        pass_on(wof[step], wos[step], nf.at[pl.ds(0, size)], ns.at[pl.ds(width, size)], w_sems, (step + 1,), keep_f, keep_s)

    for step in range(1, STEPS):
        wf[step][pl.ds(width * step, width), :] = jnp.zeros((width, B), F32)
        ws[step][pl.ds(0, width), :] = jnp.zeros((width, B), F32)

    full = cross(x_ref[...], x_ref[...])
    g0[me, 0] = full[:B, :B]
    g0[me, 1] = full[:B, B:]
    g0[me, 2] = full[B:, B:]
    pl.semaphore_wait(barrier, n_row - 1 + (k > 0).astype(jnp.int32) + (k < n_pair - 1).astype(jnp.int32))

    for step in range(STEPS):
        buf = g0 if step == 0 else gs.at[step - 1]
        if step > 0:
            total = jnp.zeros((B, B), F32)
            for c in range(CHUNKS):
                at = pl.ds(c * chunk, chunk)
                arrived(in_f(step).at[at], in_s(step).at[at], x_sems, (step, c))
                total = total + cross(in_f(step)[at, :], in_s(step)[at, :])
            buf[me] = total
        for j in range(1, n_row):
            peer_copy(buf, step, me, lax.rem(me + j, n_row)).start()
        if step > 0:
            move_w(step - 1)
        for j in range(1, n_row):
            peer_copy(buf, step, lax.rem(me + j, n_row), lax.rem(me + j, n_row)).wait_recv()
        if step == 0:
            gram_a, gram_b, gram_d = [sum((g0[i, m] for i in range(1, n_row)), g0[0, m]) for m in range(3)]
        else:
            gram_b = sum((buf[i] for i in range(1, n_row)), buf[0])
            arrived(ad_in.at[step, 0], ad_in.at[step, 1], ad_sems, (step,))
            gram_a, gram_d = ad_in[step, 0], ad_in[step, 1]
        shifts, back = turns(offs_ref, step)
        gram_a, gram_d = jacobi(gram_a, gram_b, gram_d, shifts, back, cs.at[step])
        if step == STEPS - 1:
            break
        ad_out[step, 0] = gram_a
        ad_out[step, 1] = gram_d

        def keep_a(step=step):
            ad_in[step + 1, 0] = ad_out[step, 0]

        def keep_d(step=step):
            ad_in[step + 1, 1] = ad_out[step, 0]

        pass_on(ad_out.at[step, 0], ad_out.at[step, 1], ad_in.at[step + 1, 0], ad_in.at[step + 1, 1], ad_sems, (step + 1,), keep_a, keep_d)
        for c in range(CHUNKS):
            at = pl.ds(c * chunk, chunk)
            if step == 0:
                src_f, src_s = x_ref.at[:, pl.ds(0, B)], x_ref.at[:, pl.ds(B, B)]
            else:
                src_f, src_s = in_f(step), in_s(step)
            rotate_rows(src_f, src_s, of.at[step], os_.at[step], c * chunk, chunk, cs.at[step], shifts, back)

            def keep_xf(step=step, at=at):
                in_f(step + 1)[at, :] = of[step, at, :]

            def keep_xs(step=step, at=at):
                in_s(step + 1)[at, :] = of[step, at, :]

            pass_on(
                of.at[step, at], os_.at[step, at], in_f(step + 1).at[at], in_s(step + 1).at[at],
                x_sems, (step + 1, c), keep_xf, keep_xs,
            )

    cs_out[...] = cs[STEPS - 1]
    size = width * (STEPS - 1)
    arrived(w3f.at[pl.ds(0, size)], w3s.at[pl.ds(width, size)], w_sems, (STEPS - 1,))
    for step in range(STEPS):
        buf = g0 if step == 0 else gs.at[step - 1]
        for j in range(1, n_row):
            peer_copy(buf, step, me, lax.rem(me + j, n_row)).wait_send()
        if step < STEPS - 1:
            sent(ad_out.at[step, 0], ad_out.at[step, 1], ad_sems, (step + 1,))
            sent(wof[step], wos[step], w_sems, (step + 1,))
            for c in range(CHUNKS):
                at = pl.ds(c * chunk, chunk)
                sent(of.at[step, at], os_.at[step, at], x_sems, (step + 1, c))


def last_kernel(n_pair, blocks, offs_ref, cs_ref, x3f, x3s, w3f, w3s, x_out, v_out):
    k, me, b = lax.axis_index("pair"), lax.axis_index("row"), pl.program_id(0)
    width = 2 * B
    shifts, back = turns(offs_ref, STEPS - 1)
    f, s = rotated(x3f[...], x3s[...], cs_ref, shifts, back)
    x_out[:, :B] = f
    x_out[:, B:] = s
    v_out[...] = jnp.zeros_like(v_out)
    for j in range(STEPS):
        slot = k - (STEPS - 1) + 2 * j
        slot = jnp.where(slot < 0, -1 - slot, slot)
        slot = jnp.where(slot >= n_pair, 2 * n_pair - 1 - slot, slot)

        @pl.when(slot == me * blocks + b)
        def _():
            f, s = rotated(w3f[pl.ds(j * width, width), :], w3s[pl.ds(j * width, width), :], cs_ref, shifts, back)
            v_out[:, :B] = f
            v_out[:, B:] = s


def body(n_pair, n_row, whitened, offsets):
    rows, width = whitened.shape
    v_rows = n_pair * width // n_row
    blocks = v_rows // width
    sds = functools.partial(jax.ShapeDtypeStruct, dtype=F32)
    vmem = pl.BlockSpec(memory_space=pltpu.VMEM)
    smem = pl.BlockSpec(memory_space=pltpu.SMEM)
    dma = pltpu.SemaphoreType.DMA
    x3f, x3s, w3f, w3s, cs = pl.pallas_call(
        functools.partial(main_kernel, n_pair, n_row, rows),
        out_shape=[sds((rows, B)), sds((rows, B)), sds((STEPS * width, B)), sds((STEPS * width, B)), sds((2 * ROUNDS, B))],
        in_specs=[smem, vmem],
        out_specs=[vmem] * 5,
        scratch_shapes=[
            pltpu.VMEM((STEPS - 1, rows, B), F32),
            pltpu.VMEM((STEPS - 1, rows, B), F32),
            pltpu.VMEM((STEPS - 1, rows, B), F32),
            pltpu.VMEM((STEPS - 1, rows, B), F32),
        ]
        + [pltpu.VMEM((n * width, B), F32) for n in (2, 2, 3, 3, 1, 1, 2, 2, 3, 3)]
        + [
            pltpu.VMEM((n_row, 3, B, B), F32),
            pltpu.VMEM((STEPS - 1, n_row, B, B), F32),
            pltpu.VMEM((STEPS - 1, 2, B, B), F32),
            pltpu.VMEM((STEPS, 2, B, B), F32),
            pltpu.VMEM((STEPS, 2 * ROUNDS, B), F32),
            dma((STEPS, n_row)),
            dma((STEPS, n_row)),
            dma((2, STEPS, CHUNKS)),
            dma((2, STEPS, CHUNKS)),
            dma((2, STEPS)),
            dma((2, STEPS)),
            dma((2, STEPS)),
            dma((2, STEPS)),
        ],
        compiler_params=pltpu.CompilerParams(
            collective_id=0, has_side_effects=True, vmem_limit_bytes=48 * 1024 * 1024
        ),
    )(offsets, whitened)
    piece = rows // blocks
    return pl.pallas_call(
        functools.partial(last_kernel, n_pair, blocks),
        grid=(blocks,),
        out_shape=[sds((rows, width)), sds((v_rows, width))],
        in_specs=[
            smem,
            pl.BlockSpec((2 * ROUNDS, B), lambda b: (0, 0)),
            pl.BlockSpec((piece, B), lambda b: (b, 0)),
            pl.BlockSpec((piece, B), lambda b: (b, 0)),
            pl.BlockSpec((STEPS * width, B), lambda b: (0, 0)),
            pl.BlockSpec((STEPS * width, B), lambda b: (0, 0)),
        ],
        out_specs=[pl.BlockSpec((piece, width), lambda b: (b, 0)), pl.BlockSpec((width, width), lambda b: (b, 0))],
    )(offsets, cs, x3f, x3s, w3f, w3s)


def solution(mesh):
    n_pair, n_row = mesh.shape["pair"], mesh.shape["row"]
    return jax.shard_map(
        functools.partial(body, n_pair, n_row),
        mesh=mesh,
        in_specs=(P("row", "pair"), P()),
        out_specs=(P("row", "pair"), P("row", "pair")),
        check_vma=False,
    )
```

```python
import functools

import jax
import jax.numpy as jnp
from jax import lax
from jax.experimental import pallas as pl
from jax.experimental.pallas import tpu as pltpu
from jax.sharding import PartitionSpec as P

B = 128
WIDTH = 2 * B
ROUNDS = 4
STEPS = 4
CHUNKS = 4
SETS = 14
ROWS_SENT = 4 * SETS
MESH = pl.DeviceIdType.MESH
F32 = jnp.float32

KEPT = [
    ([0, 1, 2, 3, 4], [5, 6, 7, 8, 9], [None, 10, 11, 12, 13]),
    ([0, 2], [1, 3], [None, 4]),
    ([0], [1], [None]),
]


def gram(x):
    return lax.dot_general(x, x, (((0,), (0,)), ((), ())), precision=lax.Precision.HIGHEST, preferred_element_type=F32)


def ahead(x, by):
    return pltpu.roll(x, lax.rem(B - by, B), 1)


def turns(offs_ref, step):
    offs = [offs_ref[step, r] for r in range(ROUNDS)]
    before = [jnp.int32(0)] + offs[:-1]
    return [lax.rem(b - o + B, B) for b, o in zip(before, offs)], offs[-1]


def distances(offs_ref, step):
    o = [offs_ref[step, r] for r in range(ROUNDS)]
    d1, d2, d3 = [lax.rem(b - a + B, B) for a, b in zip(o, o[1:])]
    near = [jnp.int32(0), d2, d3, d3 + d2, d3 - d2]
    far = near + [e + d1 for e in near] + [e - d1 for e in near[1:]]
    far = [lax.rem(e + 2 * B, B) for e in far]
    return o[0], (d1, d2, d3), [far, far[:5], [far[0], far[2]]]


def pick_diagonals(total, w_ref, dst_ref, offs_ref, step):
    o, _, far = distances(offs_ref, step)
    w_ref[0] = total[B:, B:]
    w_ref[1] = total[:B, B:]
    w_ref[2] = total[:B, :B]
    w_ref[3] = total[B:, :B]
    base = lax.broadcasted_iota(jnp.int32, (8, B), 0) - lax.broadcasted_iota(jnp.int32, (8, B), 1)
    for q in range(4):
        at = [lax.rem(e - o + B, B) if q == 1 else lax.rem(e + o, B) if q == 3 else e for e in far[0]]
        acc = [jnp.zeros((8, B), F32) for _ in at]
        for g in range(B // 8):
            m = w_ref[q, 8 * g : 8 * g + 8, :]
            dist = (base + 8 * g) & (B - 1)
            acc = [jnp.where(dist == t, m, v) for t, v in zip(at, acc)]
        for i, v in enumerate(acc):
            dst_ref[pl.ds(q * SETS + i, 1), :] = jnp.sum(v, axis=0, keepdims=True)
    dst_ref[pl.ds(0, 2 * SETS), :] = ahead(dst_ref[pl.ds(0, 2 * SETS), :], o)


def solve_angles(t_ref, offs_ref, step, cs_ref):
    _, turn, far = distances(offs_ref, step)
    d, e, a, b = [[t_ref[pl.ds(q * SETS + i, 1), :] for i in range(SETS)] for q in range(4)]
    for r in range(ROUNDS):
        gap = 0.5 * (d[0] - a[0])
        c0 = b[0]
        radius = jnp.sqrt(gap * gap + c0 * c0)
        sign = jnp.where(gap >= 0, 1.0, -1.0)
        t = -sign * c0 / (jnp.abs(gap) + radius + 1e-06 * (a[0] + d[0]))
        c = 1.0 / jnp.sqrt(1.0 + t * t)
        s = t * c
        cs_ref[pl.ds(r, 1), :] = c
        cs_ref[pl.ds(ROUNDS + r, 1), :] = s
        if r == ROUNDS - 1:
            break

        def partner(i):
            return (c, s) if i == 0 else (ahead(c, far[r][i]), ahead(s, far[r][i]))

        na, nb, nd, ne = [], [], [], []
        for i in KEPT[r][0]:
            cc, ss = partner(i)
            u1, u2 = cc * a[i] + ss * b[i], cc * e[i] + ss * d[i]
            v1, v2 = cc * b[i] - ss * a[i], cc * d[i] - ss * e[i]
            na.append(c * u1 + s * u2)
            nd.append(ahead(c * v2 - s * v1, turn[r]))
        for i in KEPT[r][1]:
            cc, ss = partner(i)
            v1, v2 = cc * b[i] - ss * a[i], cc * d[i] - ss * e[i]
            nb.append(c * v1 + s * v2)
        for i in KEPT[r][2]:
            if i is None:
                ne.append(nb[0])
                continue
            cc, ss = partner(i)
            u1, u2 = cc * a[i] + ss * b[i], cc * e[i] + ss * d[i]
            ne.append(ahead(c * u2 - s * u1, turn[r]))
        a, b, d, e = na, nb, nd, ne


def rotated(f, s, cs_ref, turn):
    shifts, back = turn
    for r in range(ROUNDS):
        s = pltpu.roll(s, shifts[r], 1)
        c = cs_ref[pl.ds(r, 1), :]
        n = cs_ref[pl.ds(ROUNDS + r, 1), :]
        f, s = f * c + s * n, s * c - f * n
    return f, pltpu.roll(s, back, 1)


def main_kernel(
    n_pair, n_row, rows, offs_hbm, x_hbm, x_out, w_out,
    offs_ref, x_in, xf, xs, of, os_, w_ref, gs, tot, cs, hl, hr, le, re,
    r0l, l0l, r0r, l0r, r1, l1, edge0, edge1, w3f, w3s,
    in_sem, g_send, g_recv, x_send, x_recv, h_send, h_recv,
):
    k = lax.axis_index("pair")
    me = lax.axis_index("row")
    first, last = k == 0, k == n_pair - 1
    chunk = rows // CHUNKS

    fetch_offs = pltpu.make_async_copy(offs_hbm, offs_ref, in_sem.at[CHUNKS])
    fetch_offs.start()
    fetch = [
        pltpu.make_async_copy(x_hbm.at[pl.ds(c * chunk, chunk)], x_in.at[pl.ds(c * chunk, chunk)], in_sem.at[c])
        for c in range(CHUNKS)
    ]
    for copy in fetch:
        copy.start()

    barrier = pltpu.get_barrier_semaphore()

    @pl.when(k > 0)
    def _():
        pl.semaphore_signal(barrier, inc=1, device_id={"pair": k - 1}, device_id_type=MESH)

    @pl.when(k < n_pair - 1)
    def _():
        pl.semaphore_signal(barrier, inc=1, device_id={"pair": k + 1}, device_id_type=MESH)

    for j in range(1, n_row):
        pl.semaphore_signal(barrier, inc=1, device_id={"row": lax.rem(me + j, n_row)}, device_id_type=MESH)

    def to_right(src, dst, sems, at):
        return pltpu.make_async_remote_copy(
            src_ref=src, dst_ref=dst, send_sem=sems[0].at[(0,) + at], recv_sem=sems[1].at[(0,) + at],
            device_id={"pair": k + 1}, device_id_type=MESH,
        )

    def to_left(src, dst, sems, at):
        return pltpu.make_async_remote_copy(
            src_ref=src, dst_ref=dst, send_sem=sems[0].at[(1,) + at], recv_sem=sems[1].at[(1,) + at],
            device_id={"pair": k - 1}, device_id_type=MESH,
        )

    def arrived(dst_l, dst_r, sems, at):
        @pl.when(k > 0)
        def _():
            to_right(dst_l, dst_l, sems, at).wait_recv()

        @pl.when(k < n_pair - 1)
        def _():
            to_left(dst_r, dst_r, sems, at).wait_recv()

    def sent(src_r, src_l, sems, at):
        @pl.when(k < n_pair - 1)
        def _():
            to_right(src_r, src_r, sems, at).wait_send()

        @pl.when(k > 0)
        def _():
            to_left(src_l, src_l, sems, at).wait_send()

    def peer_copy(step, slot, to):
        return pltpu.make_async_remote_copy(
            src_ref=gs.at[step, slot], dst_ref=gs.at[step, slot], send_sem=g_send.at[step, to],
            recv_sem=g_recv.at[step, slot], device_id={"row": to}, device_id_type=MESH,
        )

    x_sems, h_sems = (x_send, x_recv), (h_send, h_recv)

    def send_rows(step, c):
        at = pl.ds(c * chunk, chunk)
        f, s = of.at[step, at], os_.at[step, at]
        new_f, new_s = xf.at[step, at], xs.at[step, at]

        @pl.when(first)
        def _():
            to_right(s, new_f, x_sems, (step, c)).start()
            new_f[...] = f[...]

        @pl.when(jnp.logical_and(k > 0, k < n_pair - 1))
        def _():
            to_right(f, new_f, x_sems, (step, c)).start()

        @pl.when(last)
        def _():
            new_s[...] = f[...]

        @pl.when(k > 0)
        def _():
            to_left(s, new_s, x_sems, (step, c)).start()

    def send_history(step):
        if step > 0:
            le[step, pl.ds(0, step)] = hl[step - 1, pl.ds(0, step)]
            re[step, pl.ds(0, step)] = hr[step - 1, pl.ds(0, step)]
        le[step, step] = cs[step]
        re[step, step] = cs[step]
        n = pl.ds(0, step + 1)

        @pl.when(k < n_pair - 1)
        def _():
            to_right(le.at[step, n], hl.at[step, n], h_sems, (step,)).start()

        @pl.when(k > 0)
        def _():
            to_left(re.at[step, n], hr.at[step, n], h_sems, (step,)).start()

        @pl.when(first)
        def _():
            hl[step, n] = re[step, n]

        @pl.when(last)
        def _():
            hr[step, n] = le[step, n]

    def history_arrived(step):
        n = pl.ds(0, step + 1)
        arrived(hl.at[step, n], hr.at[step, n], h_sems, (step,))

    def node(level, slot, cs_ref, from_left, from_right, dst_right, dst_left):
        turn = turns(offs_ref, level)
        outside = jnp.logical_or(slot < 0, slot >= n_pair)
        swap = jnp.logical_or(jnp.logical_or(slot < -1, slot == 0), slot >= n_pair)
        for g in range(level + 1):
            at = pl.ds(g * WIDTH, WIDTH)
            if level == 0:
                row = lax.broadcasted_iota(jnp.int32, (WIDTH, B), 0)
                col = lax.broadcasted_iota(jnp.int32, (WIDTH, B), 1)
                f, s = [jnp.where(row == col + h, 1.0, 0.0).astype(F32) for h in (0, B)]
            else:
                zero = jnp.zeros((WIDTH, B), F32)
                p = from_left[at, :] if g < level else zero
                q = from_right[pl.ds((g - 1) * WIDTH, WIDTH), :] if g > 0 else zero
                f, s = jnp.where(outside, q, p), jnp.where(outside, p, q)
            f, s = rotated(f, s, cs_ref, turn)
            if dst_right is not None:
                dst_right[at, :] = jnp.where(swap, s, f)
            if dst_left is not None:
                dst_left[at, :] = jnp.where(swap, f, s)

    total = jnp.zeros((WIDTH, WIDTH), F32)
    for c in range(CHUNKS):
        fetch[c].wait()
        total = total + gram(x_in[pl.ds(c * chunk, chunk), :])
    fetch_offs.wait()
    for step in range(STEPS):
        if step > 0:
            history_arrived(step - 1)
            if step == 1:
                node(0, k - 1, hl.at[0, 0], None, None, r0l, l0l)
                node(0, k + 1, hr.at[0, 0], None, None, r0r, l0r)
            if step == 2:
                node(1, k, cs.at[1], r0l, l0r, r1, l1)
            if step == 3:
                node(0, k - 3, hl.at[2, 0], None, None, edge0, None)
                node(1, k - 2, hl.at[2, 1], edge0, l0l, edge1, None)
                node(2, k - 1, hl.at[2, 2], edge1, l1, w3f, None)
                node(0, k + 3, hr.at[2, 0], None, None, None, edge0)
                node(1, k + 2, hr.at[2, 1], r0r, edge0, None, edge1)
                node(2, k + 1, hr.at[2, 2], r1, edge1, None, w3s)
            total = jnp.zeros((WIDTH, WIDTH), F32)
            for c in range(CHUNKS):
                at = pl.ds(c * chunk, chunk)
                arrived(xf.at[step - 1, at], xs.at[step - 1, at], x_sems, (step - 1, c))
                total = total + gram(jnp.concatenate([xf[step - 1, at, :], xs[step - 1, at, :]], axis=1))
        pick_diagonals(total, w_ref, gs.at[step, me], offs_ref, step)
        if step == 0:
            pl.semaphore_wait(barrier, n_row - 1 + (k > 0).astype(jnp.int32) + (k < n_pair - 1).astype(jnp.int32))
        for j in range(1, n_row):
            peer_copy(step, me, lax.rem(me + j, n_row)).start()
        for j in range(1, n_row):
            peer_copy(step, lax.rem(me + j, n_row), lax.rem(me + j, n_row)).wait_recv()
        tot[...] = sum((gs[step, i] for i in range(1, n_row)), gs[step, 0])
        solve_angles(tot, offs_ref, step, cs.at[step])
        turn = turns(offs_ref, step)
        if step < STEPS - 1:
            send_history(step)
        for c in range(CHUNKS):
            at = pl.ds(c * chunk, chunk)
            if step == 0:
                f, s = x_in[at, :B], x_in[at, B:]
            else:
                f, s = xf[step - 1, at, :], xs[step - 1, at, :]
            f, s = rotated(f, s, cs.at[step], turn)
            if step < STEPS - 1:
                of[step, at, :] = f
                os_[step, at, :] = s
                send_rows(step, c)
            else:
                x_out[at, :B] = f
                x_out[at, B:] = s

    turn = turns(offs_ref, STEPS - 1)
    for g in range(STEPS):
        at = pl.ds(g * WIDTH, WIDTH)
        zero = jnp.zeros((WIDTH, B), F32)
        f = w3f[at, :] if g < STEPS - 1 else zero
        s = w3s[pl.ds((g - 1) * WIDTH, WIDTH), :] if g > 0 else zero
        f, s = rotated(f, s, cs.at[STEPS - 1], turn)
        w_out[at, :B] = f
        w_out[at, B:] = s

    for step in range(STEPS):
        for j in range(1, n_row):
            peer_copy(step, me, lax.rem(me + j, n_row)).wait_send()
        if step < STEPS - 1:
            n = pl.ds(0, step + 1)
            sent(le.at[step, n], re.at[step, n], h_sems, (step,))
            for c in range(CHUNKS):
                at = pl.ds(c * chunk, chunk)
                sent(of.at[step, at], os_.at[step, at], x_sems, (step, c))


def place_kernel(n_pair, blocks, x_ref, w_ref, x_out, v_out, zero, sem):
    k, me = lax.axis_index("pair"), lax.axis_index("row")
    move_x = pltpu.make_async_copy(x_ref, x_out, sem.at[blocks + STEPS])
    move_x.start()
    zero[...] = jnp.zeros_like(zero)
    slots = []
    for j in range(STEPS):
        slot = k - (STEPS - 1) + 2 * j
        slot = jnp.where(slot < 0, -1 - slot, slot)
        slots.append(jnp.where(slot >= n_pair, 2 * n_pair - 1 - slot, slot) - me * blocks)

    def piece(j):
        here = jnp.logical_and(slots[j] >= 0, slots[j] < blocks)
        place = pl.multiple_of(jnp.where(here, slots[j], 0) * WIDTH, WIDTH)
        return here, pltpu.make_async_copy(
            w_ref.at[pl.ds(j * WIDTH, WIDTH)], v_out.at[pl.ds(place, WIDTH)], sem.at[blocks + j]
        )

    def blank(b):
        empty = slots[0] != b
        for j in range(1, STEPS):
            empty = jnp.logical_and(empty, slots[j] != b)
        return empty, pltpu.make_async_copy(zero, v_out.at[pl.ds(b * WIDTH, WIDTH)], sem.at[b])

    moves = [piece(j) for j in range(STEPS)] + [blank(b) for b in range(blocks)]
    for needed, copy in moves:
        pl.when(needed)(copy.start)
    for needed, copy in moves:
        pl.when(needed)(copy.wait)
    move_x.wait()


def body(n_pair, n_row, whitened, offsets):
    rows, width = whitened.shape
    v_rows = n_pair * width // n_row
    blocks = v_rows // width
    sds = functools.partial(jax.ShapeDtypeStruct, dtype=F32)
    vmem = pl.BlockSpec(memory_space=pltpu.VMEM)
    anywhere = pl.BlockSpec(memory_space=pl.ANY)
    dma = pltpu.SemaphoreType.DMA

    def held(*shape):
        return pltpu.VMEM(shape, F32)

    x_last, w_last = pl.pallas_call(
        functools.partial(main_kernel, n_pair, n_row, rows),
        out_shape=[sds((rows, width)), sds((STEPS * width, width))],
        in_specs=[anywhere, anywhere],
        out_specs=[vmem, vmem],
        scratch_shapes=[
            pltpu.SMEM((STEPS, ROUNDS), jnp.int32),
            held(rows, width),
            held(STEPS - 1, rows, B),
            held(STEPS - 1, rows, B),
            held(STEPS - 1, rows, B),
            held(STEPS - 1, rows, B),
            held(4, B, B),
            held(STEPS, n_row, ROWS_SENT, B),
            held(ROWS_SENT, B),
            held(STEPS, 2 * ROUNDS, B),
        ]
        + [held(STEPS - 1, STEPS - 1, 2 * ROUNDS, B) for _ in range(4)]
        + [held(n * width, B) for n in (1, 1, 1, 1, 2, 2, 1, 2, 3, 3)]
        + [
            dma((CHUNKS + 1,)),
            dma((STEPS, n_row)),
            dma((STEPS, n_row)),
            dma((2, STEPS - 1, CHUNKS)),
            dma((2, STEPS - 1, CHUNKS)),
            dma((2, STEPS - 1)),
            dma((2, STEPS - 1)),
        ],
        compiler_params=pltpu.CompilerParams(
            collective_id=0, has_side_effects=True, vmem_limit_bytes=40 * 1024 * 1024
        ),
    )(offsets, whitened)
    return pl.pallas_call(
        functools.partial(place_kernel, n_pair, blocks),
        out_shape=[sds((rows, width)), sds((v_rows, width))],
        in_specs=[vmem, vmem],
        out_specs=[anywhere, anywhere],
        scratch_shapes=[held(width, width), dma((blocks + STEPS + 1,))],
    )(x_last, w_last)


def solution(mesh):
    n_pair, n_row = mesh.shape["pair"], mesh.shape["row"]
    return jax.shard_map(
        functools.partial(body, n_pair, n_row),
        mesh=mesh,
        in_specs=(P("row", "pair"), P()),
        out_specs=(P("row", "pair"), P("row", "pair")),
        check_vma=False,
    )
```

```python
import functools

import jax
import jax.numpy as jnp
from jax import lax
from jax.experimental import pallas as pl
from jax.experimental.pallas import tpu as pltpu
from jax.sharding import PartitionSpec as P

B = 128
WIDTH = 2 * B
ROUNDS = 4
STEPS = 4
FETCHES = 4
LATE = 3
EARLY = 7
SETS = 14
ROWS_SENT = 4 * SETS
MESH = pl.DeviceIdType.MESH
F32 = jnp.float32

KEPT = [
    ([0, 1, 2, 3, 4], [5, 6, 7, 8, 9], [None, 10, 11, 12, 13]),
    ([0, 2], [1, 3], [None, 4]),
    ([0], [1], [None]),
]


def gram(x):
    return lax.dot_general(x, x, (((0,), (0,)), ((), ())), precision=lax.Precision.HIGHEST, preferred_element_type=F32)


def ahead(x, by):
    return pltpu.roll(x, lax.rem(B - by, B), 1)


def turns(offs_ref, step):
    offs = [offs_ref[step, r] for r in range(ROUNDS)]
    before = [jnp.int32(0)] + offs[:-1]
    return [lax.rem(b - o + B, B) for b, o in zip(before, offs)], offs[-1]


def distances(offs_ref, step):
    o = [offs_ref[step, r] for r in range(ROUNDS)]
    d1, d2, d3 = [lax.rem(b - a + B, B) for a, b in zip(o, o[1:])]
    near = [jnp.int32(0), d2, d3, d3 + d2, d3 - d2]
    far = near + [e + d1 for e in near] + [e - d1 for e in near[1:]]
    far = [lax.rem(e + 2 * B, B) for e in far]
    return o[0], (d1, d2, d3), [far, far[:5], [far[0], far[2]]]


def pick_diagonals(total, w_ref, dst_ref, offs_ref, step):
    o, _, far = distances(offs_ref, step)
    w_ref[0] = total[B:, B:]
    w_ref[1] = total[:B, B:]
    w_ref[2] = total[:B, :B]
    w_ref[3] = total[B:, :B]
    base = lax.broadcasted_iota(jnp.int32, (8, B), 0) - lax.broadcasted_iota(jnp.int32, (8, B), 1)
    for q in range(4):
        at = [lax.rem(e - o + B, B) if q == 1 else lax.rem(e + o, B) if q == 3 else e for e in far[0]]
        acc = [jnp.zeros((8, B), F32) for _ in at]
        for g in range(B // 8):
            m = w_ref[q, 8 * g : 8 * g + 8, :]
            dist = (base + 8 * g) & (B - 1)
            acc = [jnp.where(dist == t, m, v) for t, v in zip(at, acc)]
        for i, v in enumerate(acc):
            dst_ref[pl.ds(q * SETS + i, 1), :] = jnp.sum(v, axis=0, keepdims=True)
    dst_ref[pl.ds(0, 2 * SETS), :] = ahead(dst_ref[pl.ds(0, 2 * SETS), :], o)


def solve_angles(t_ref, offs_ref, step, cs_ref):
    _, turn, far = distances(offs_ref, step)
    d, e, a, b = [[t_ref[pl.ds(q * SETS + i, 1), :] for i in range(SETS)] for q in range(4)]
    for r in range(ROUNDS):
        gap = 0.5 * (d[0] - a[0])
        c0 = b[0]
        radius = jnp.sqrt(gap * gap + c0 * c0)
        sign = jnp.where(gap >= 0, 1.0, -1.0)
        t = -sign * c0 / (jnp.abs(gap) + radius + 1e-06 * (a[0] + d[0]))
        c = 1.0 / jnp.sqrt(1.0 + t * t)
        s = t * c
        cs_ref[pl.ds(r, 1), :] = c
        cs_ref[pl.ds(ROUNDS + r, 1), :] = s
        if r == ROUNDS - 1:
            break

        def partner(i):
            return (c, s) if i == 0 else (ahead(c, far[r][i]), ahead(s, far[r][i]))

        na, nb, nd, ne = [], [], [], []
        for i in KEPT[r][0]:
            cc, ss = partner(i)
            u1, u2 = cc * a[i] + ss * b[i], cc * e[i] + ss * d[i]
            v1, v2 = cc * b[i] - ss * a[i], cc * d[i] - ss * e[i]
            na.append(c * u1 + s * u2)
            nd.append(ahead(c * v2 - s * v1, turn[r]))
        for i in KEPT[r][1]:
            cc, ss = partner(i)
            v1, v2 = cc * b[i] - ss * a[i], cc * d[i] - ss * e[i]
            nb.append(c * v1 + s * v2)
        for i in KEPT[r][2]:
            if i is None:
                ne.append(nb[0])
                continue
            cc, ss = partner(i)
            u1, u2 = cc * a[i] + ss * b[i], cc * e[i] + ss * d[i]
            ne.append(ahead(c * u2 - s * u1, turn[r]))
        a, b, d, e = na, nb, nd, ne


def rotated(f, s, cs_ref, turn):
    shifts, back = turn
    for r in range(ROUNDS):
        s = pltpu.roll(s, shifts[r], 1)
        c = cs_ref[pl.ds(r, 1), :]
        n = cs_ref[pl.ds(ROUNDS + r, 1), :]
        f, s = f * c + s * n, s * c - f * n
    return f, pltpu.roll(s, back, 1)


def main_kernel(
    n_pair, n_row, rows, early, offs_hbm, x_hbm, x_out, w_out,
    offs_ref, x_in, xf, xs, of, os_, el, er, w_ref, gs, tot, cs, hl, hr, le, re,
    r0l, l0l, r0r, l0r, r1, l1, edge0, edge1, w3f, w3s,
    in_sem, g_send, g_recv, x_send, x_recv, e_send, e_recv, h_send, h_recv,
):
    k = lax.axis_index("pair")
    me = lax.axis_index("row")
    first, last = k == 0, k == n_pair - 1
    piece = rows // FETCHES
    late = (rows - early) // LATE
    top = pl.ds(0, early)

    fetch_offs = pltpu.make_async_copy(offs_hbm, offs_ref, in_sem.at[FETCHES])
    fetch_offs.start()
    fetch = [
        pltpu.make_async_copy(x_hbm.at[pl.ds(c * piece, piece)], x_in.at[pl.ds(c * piece, piece)], in_sem.at[c])
        for c in range(FETCHES)
    ]
    for copy in fetch:
        copy.start()

    barrier = pltpu.get_barrier_semaphore()

    @pl.when(k > 0)
    def _():
        pl.semaphore_signal(barrier, inc=1, device_id={"pair": k - 1}, device_id_type=MESH)

    @pl.when(k < n_pair - 1)
    def _():
        pl.semaphore_signal(barrier, inc=1, device_id={"pair": k + 1}, device_id_type=MESH)

    for j in range(1, n_row):
        pl.semaphore_signal(barrier, inc=1, device_id={"row": lax.rem(me + j, n_row)}, device_id_type=MESH)

    def to_right(src, dst, sems, at):
        return pltpu.make_async_remote_copy(
            src_ref=src, dst_ref=dst, send_sem=sems[0].at[(0,) + at], recv_sem=sems[1].at[(0,) + at],
            device_id={"pair": k + 1}, device_id_type=MESH,
        )

    def to_left(src, dst, sems, at):
        return pltpu.make_async_remote_copy(
            src_ref=src, dst_ref=dst, send_sem=sems[0].at[(1,) + at], recv_sem=sems[1].at[(1,) + at],
            device_id={"pair": k - 1}, device_id_type=MESH,
        )

    def arrived(dst_l, dst_r, sems, at):
        @pl.when(k > 0)
        def _():
            to_right(dst_l, dst_l, sems, at).wait_recv()

        @pl.when(k < n_pair - 1)
        def _():
            to_left(dst_r, dst_r, sems, at).wait_recv()

    def sent(src_r, src_l, sems, at):
        @pl.when(k < n_pair - 1)
        def _():
            to_right(src_r, src_r, sems, at).wait_send()

        @pl.when(k > 0)
        def _():
            to_left(src_l, src_l, sems, at).wait_send()

    def peer_copy(step, slot, to):
        return pltpu.make_async_remote_copy(
            src_ref=gs.at[step, slot], dst_ref=gs.at[step, slot], send_sem=g_send.at[step, to],
            recv_sem=g_recv.at[step, slot], device_id={"row": to}, device_id_type=MESH,
        )

    x_sems, e_sems, h_sems = (x_send, x_recv), (e_send, e_recv), (h_send, h_recv)

    def late_rows(c):
        return pl.ds(early + c * late, late)

    def send_late(step, c):
        at = late_rows(c)
        f, s = of.at[step, at], os_.at[step, at]
        new_f, new_s = xf.at[step, at], xs.at[step, at]

        @pl.when(first)
        def _():
            to_right(s, new_f, x_sems, (step, c)).start()
            new_f[...] = f[...]

        @pl.when(jnp.logical_and(k > 0, k < n_pair - 1))
        def _():
            to_right(f, new_f, x_sems, (step, c)).start()

        @pl.when(last)
        def _():
            new_s[...] = f[...]

        @pl.when(k > 0)
        def _():
            to_left(s, new_s, x_sems, (step, c)).start()

    def early_source(step, h):
        if step == 0:
            return x_in.at[top, pl.ds(h * B, B)]
        return (xf, xs)[h].at[step - 1, top]

    def send_early(step):
        for h in range(2):
            src = early_source(step, h)

            @pl.when(k < n_pair - 1)
            def _():
                to_right(src, el.at[step, h], e_sems, (step, h)).start()

            @pl.when(k > 0)
            def _():
                to_left(src, er.at[step, h], e_sems, (step, h)).start()

            @pl.when(first)
            def _():
                el[step, h] = src[...]

            @pl.when(last)
            def _():
                er[step, h] = src[...]

    def rotate_early(step):
        turn = turns(offs_ref, step)
        f, s = rotated(el[step, 0], el[step, 1], hl.at[step, step], turn)
        xf[step, top, :] = jnp.where(k == 1, s, f)
        f, s = rotated(er[step, 0], er[step, 1], hr.at[step, step], turn)
        xs[step, top, :] = jnp.where(last, f, s)

    def send_history(step):
        if step > 0:
            le[step, pl.ds(0, step)] = hl[step - 1, pl.ds(0, step)]
            re[step, pl.ds(0, step)] = hr[step - 1, pl.ds(0, step)]
        le[step, step] = cs[step]
        re[step, step] = cs[step]
        n = pl.ds(0, step + 1)

        @pl.when(k < n_pair - 1)
        def _():
            to_right(le.at[step, n], hl.at[step, n], h_sems, (step,)).start()

        @pl.when(k > 0)
        def _():
            to_left(re.at[step, n], hr.at[step, n], h_sems, (step,)).start()

        @pl.when(first)
        def _():
            hl[step, n] = re[step, n]

        @pl.when(last)
        def _():
            hr[step, n] = le[step, n]

    def node(level, slot, cs_ref, from_left, from_right, dst_right, dst_left):
        turn = turns(offs_ref, level)
        outside = jnp.logical_or(slot < 0, slot >= n_pair)
        swap = jnp.logical_or(jnp.logical_or(slot < -1, slot == 0), slot >= n_pair)
        if level == 0:
            row = lax.broadcasted_iota(jnp.int32, (WIDTH, B), 0)
            col = lax.broadcasted_iota(jnp.int32, (WIDTH, B), 1)
            f, s = [jnp.where(row == col + h, 1.0, 0.0).astype(F32) for h in (0, B)]
        else:
            zero = jnp.zeros((WIDTH, B), F32)
            p = jnp.concatenate([from_left[...], zero], axis=0)
            q = jnp.concatenate([zero, from_right[...]], axis=0)
            f, s = jnp.where(outside, q, p), jnp.where(outside, p, q)
        f, s = rotated(f, s, cs_ref, turn)
        if dst_right is not None:
            dst_right[...] = jnp.where(swap, s, f)
        if dst_left is not None:
            dst_left[...] = jnp.where(swap, f, s)

    def rebuild(step):
        if step == 1:
            node(0, k - 1, hl.at[0, 0], None, None, r0l, l0l)
            node(0, k + 1, hr.at[0, 0], None, None, r0r, l0r)
        if step == 2:
            node(1, k, cs.at[1], r0l, l0r, r1, l1)
        if step == 3:
            node(0, k - 3, hl.at[2, 0], None, None, edge0.at[0], None)
            node(0, k + 3, hr.at[2, 0], None, None, None, edge0.at[1])
            node(1, k - 2, hl.at[2, 1], edge0.at[0], l0l, edge1.at[0], None)
            node(1, k + 2, hr.at[2, 1], r0r, edge0.at[1], None, edge1.at[1])
            node(2, k - 1, hl.at[2, 2], edge1.at[0], l1, w3f, None)
            node(2, k + 1, hr.at[2, 2], r1, edge1.at[1], None, w3s)

    for copy in fetch:
        copy.wait()
    pl.semaphore_wait(barrier, n_row - 1 + (k > 0).astype(jnp.int32) + (k < n_pair - 1).astype(jnp.int32))
    send_early(0)
    total = gram(x_in[...])
    fetch_offs.wait()
    for step in range(STEPS):
        pick_diagonals(total, w_ref, gs.at[step, me], offs_ref, step)
        for j in range(1, n_row):
            peer_copy(step, me, lax.rem(me + j, n_row)).start()
        rebuild(step)
        for j in range(1, n_row):
            peer_copy(step, lax.rem(me + j, n_row), lax.rem(me + j, n_row)).wait_recv()
        tot[...] = sum((gs[step, i] for i in range(1, n_row)), gs[step, 0])
        solve_angles(tot, offs_ref, step, cs.at[step])
        if step == STEPS - 1:
            break
        turn = turns(offs_ref, step)
        send_history(step)
        for c in range(LATE):
            at = late_rows(c)
            if step == 0:
                f, s = x_in[at, :B], x_in[at, B:]
            else:
                f, s = xf[step - 1, at, :], xs[step - 1, at, :]
            f, s = rotated(f, s, cs.at[step], turn)
            of[step, at, :] = f
            os_[step, at, :] = s
            send_late(step, c)
        n = pl.ds(0, step + 1)
        arrived(hl.at[step, n], hr.at[step, n], h_sems, (step,))
        for h in range(2):
            arrived(el.at[step, h], er.at[step, h], e_sems, (step, h))
        rotate_early(step)
        total = gram(jnp.concatenate([xf[step, top, :], xs[step, top, :]], axis=1))
        for c in range(LATE):
            at = late_rows(c)
            arrived(xf.at[step, at], xs.at[step, at], x_sems, (step, c))
            if c == LATE - 1 and step + 1 < STEPS - 1:
                send_early(step + 1)
            total = total + gram(jnp.concatenate([xf[step, at, :], xs[step, at, :]], axis=1))

    turn = turns(offs_ref, STEPS - 1)
    for g in range(2):
        at = pl.ds(g * (rows // 2), rows // 2)
        f, s = rotated(xf[STEPS - 2, at, :], xs[STEPS - 2, at, :], cs.at[STEPS - 1], turn)
        x_out[at, :B] = f
        x_out[at, B:] = s
    zero = jnp.zeros((WIDTH, B), F32)
    w_out_rows = [
        (w3f[: 2 * WIDTH, :], jnp.concatenate([zero, w3s[:WIDTH, :]], axis=0)),
        (jnp.concatenate([w3f[2 * WIDTH :, :], zero], axis=0), w3s[WIDTH:, :]),
    ]
    for g, (f, s) in enumerate(w_out_rows):
        at = pl.ds(g * 2 * WIDTH, 2 * WIDTH)
        f, s = rotated(f, s, cs.at[STEPS - 1], turn)
        w_out[at, :B] = f
        w_out[at, B:] = s

    for step in range(STEPS):
        for j in range(1, n_row):
            peer_copy(step, me, lax.rem(me + j, n_row)).wait_send()
        if step < STEPS - 1:
            n = pl.ds(0, step + 1)
            sent(le.at[step, n], re.at[step, n], h_sems, (step,))
            for h in range(2):
                sent(early_source(step, h), early_source(step, h), e_sems, (step, h))
            for c in range(LATE):
                at = late_rows(c)
                sent(of.at[step, at], os_.at[step, at], x_sems, (step, c))


def place_kernel(n_pair, blocks, x_ref, w_ref, x_out, v_out, zero, sem):
    k, me = lax.axis_index("pair"), lax.axis_index("row")
    move_x = pltpu.make_async_copy(x_ref, x_out, sem.at[blocks + STEPS])
    move_x.start()
    zero[...] = jnp.zeros_like(zero)
    slots = []
    for j in range(STEPS):
        slot = k - (STEPS - 1) + 2 * j
        slot = jnp.where(slot < 0, -1 - slot, slot)
        slots.append(jnp.where(slot >= n_pair, 2 * n_pair - 1 - slot, slot) - me * blocks)

    def piece(j):
        here = jnp.logical_and(slots[j] >= 0, slots[j] < blocks)
        place = pl.multiple_of(jnp.where(here, slots[j], 0) * WIDTH, WIDTH)
        return here, pltpu.make_async_copy(
            w_ref.at[pl.ds(j * WIDTH, WIDTH)], v_out.at[pl.ds(place, WIDTH)], sem.at[blocks + j]
        )

    def blank(b):
        empty = slots[0] != b
        for j in range(1, STEPS):
            empty = jnp.logical_and(empty, slots[j] != b)
        return empty, pltpu.make_async_copy(zero, v_out.at[pl.ds(b * WIDTH, WIDTH)], sem.at[b])

    moves = [piece(j) for j in range(STEPS)] + [blank(b) for b in range(blocks)]
    for needed, copy in moves:
        pl.when(needed)(copy.start)
    for needed, copy in moves:
        pl.when(needed)(copy.wait)
    move_x.wait()


def body(n_pair, n_row, whitened, offsets):
    rows, width = whitened.shape
    v_rows = n_pair * width // n_row
    blocks = v_rows // width
    early = rows * EARLY // 16
    sds = functools.partial(jax.ShapeDtypeStruct, dtype=F32)
    vmem = pl.BlockSpec(memory_space=pltpu.VMEM)
    anywhere = pl.BlockSpec(memory_space=pl.ANY)
    hbm = pl.BlockSpec(memory_space=pltpu.HBM)
    dma = pltpu.SemaphoreType.DMA

    def held(*shape):
        return pltpu.VMEM(shape, F32)

    x_last, w_last = pl.pallas_call(
        functools.partial(main_kernel, n_pair, n_row, rows, early),
        out_shape=[sds((rows, width)), sds((STEPS * width, width))],
        in_specs=[hbm, hbm],
        out_specs=[vmem, vmem],
        scratch_shapes=[
            pltpu.SMEM((STEPS, ROUNDS), jnp.int32),
            held(rows, width),
            held(STEPS - 1, rows, B),
            held(STEPS - 1, rows, B),
            held(STEPS - 1, rows, B),
            held(STEPS - 1, rows, B),
            held(STEPS - 1, 2, early, B),
            held(STEPS - 1, 2, early, B),
            held(4, B, B),
            held(STEPS, n_row, ROWS_SENT, B),
            held(ROWS_SENT, B),
            held(STEPS, 2 * ROUNDS, B),
        ]
        + [held(STEPS - 1, STEPS - 1, 2 * ROUNDS, B) for _ in range(4)]
        + [held(n * width, B) for n in (1, 1, 1, 1, 2, 2)]
        + [held(2, width, B), held(2, 2 * width, B), held(3 * width, B), held(3 * width, B)]
        + [
            dma((FETCHES + 1,)),
            dma((STEPS, n_row)),
            dma((STEPS, n_row)),
            dma((2, STEPS - 1, LATE)),
            dma((2, STEPS - 1, LATE)),
            dma((2, STEPS - 1, 2)),
            dma((2, STEPS - 1, 2)),
            dma((2, STEPS - 1)),
            dma((2, STEPS - 1)),
        ],
        compiler_params=pltpu.CompilerParams(
            collective_id=0, has_side_effects=True, vmem_limit_bytes=40 * 1024 * 1024
        ),
    )(pltpu.with_memory_space_constraint(offsets, pltpu.HBM), pltpu.with_memory_space_constraint(whitened, pltpu.HBM))
    return pl.pallas_call(
        functools.partial(place_kernel, n_pair, blocks),
        out_shape=[sds((rows, width)), sds((v_rows, width))],
        in_specs=[vmem, vmem],
        out_specs=[anywhere, anywhere],
        scratch_shapes=[held(width, width), dma((blocks + STEPS + 1,))],
        compiler_params=pltpu.CompilerParams(vmem_limit_bytes=4 * 1024 * 1024),
    )(x_last, w_last)


def solution(mesh):
    n_pair, n_row = mesh.shape["pair"], mesh.shape["row"]
    return jax.shard_map(
        functools.partial(body, n_pair, n_row),
        mesh=mesh,
        in_specs=(P("row", "pair"), P()),
        out_specs=(P("row", "pair"), P("row", "pair")),
        check_vma=False,
    )
```

```python
import functools

import jax
import jax.numpy as jnp
from jax import lax
from jax.experimental import pallas as pl
from jax.experimental.pallas import tpu as pltpu
from jax.sharding import PartitionSpec as P

B = 128
WIDTH = 2 * B
ROUNDS = 4
STEPS = 4
FETCHES = 4
EARLY = (7, 12, 12)
LATE = ((4, 6, 4, 4), (6, 2), (6, 2))
SETS = 14
ROWS_SENT = 4 * SETS
MESH = pl.DeviceIdType.MESH
F32 = jnp.float32

KEPT = [
    ([0, 1, 2, 3, 4], [5, 6, 7, 8, 9], [None, 10, 11, 12, 13]),
    ([0, 2], [1, 3], [None, 4]),
    ([0], [1], [None]),
]


def gram(x):
    return lax.dot_general(x, x, (((0,), (0,)), ((), ())), precision=lax.Precision.HIGHEST, preferred_element_type=F32)


def ahead(x, by):
    return pltpu.roll(x, lax.rem(B - by, B), 1)


def turns(offs_ref, step):
    offs = [offs_ref[step, r] for r in range(ROUNDS)]
    before = [jnp.int32(0)] + offs[:-1]
    return [lax.rem(b - o + B, B) for b, o in zip(before, offs)], offs[-1]


def distances(offs_ref, step):
    o = [offs_ref[step, r] for r in range(ROUNDS)]
    d1, d2, d3 = [lax.rem(b - a + B, B) for a, b in zip(o, o[1:])]
    near = [jnp.int32(0), d2, d3, d3 + d2, d3 - d2]
    far = near + [e + d1 for e in near] + [e - d1 for e in near[1:]]
    far = [lax.rem(e + 2 * B, B) for e in far]
    return o[0], (d1, d2, d3), [far, far[:5], [far[0], far[2]]]


def pick_diagonals(total, w_ref, dst_ref, offs_ref, step):
    o, _, far = distances(offs_ref, step)
    w_ref[0] = total[B:, B:]
    w_ref[1] = total[:B, B:]
    w_ref[2] = total[:B, :B]
    w_ref[3] = total[B:, :B]
    base = lax.broadcasted_iota(jnp.int32, (8, B), 0) - lax.broadcasted_iota(jnp.int32, (8, B), 1)
    same, to_first, to_second = far[0], [lax.rem(e - o + B, B) for e in far[0]], [lax.rem(e + o, B) for e in far[0]]
    for at, blocks in ((same, (0, 2)), (to_first, (1,)), (to_second, (3,))):
        acc = [[jnp.zeros((8, B), F32) for _ in at] for _ in blocks]
        for g in range(B // 8):
            dist = (base + 8 * g) & (B - 1)
            m = [w_ref[q, 8 * g : 8 * g + 8, :] for q in blocks]
            for i, t in enumerate(at):
                here = dist == t
                for n in range(len(blocks)):
                    acc[n][i] = jnp.where(here, m[n], acc[n][i])
        for n, q in enumerate(blocks):
            for i, v in enumerate(acc[n]):
                dst_ref[pl.ds(q * SETS + i, 1), :] = jnp.sum(v, axis=0, keepdims=True)
    dst_ref[pl.ds(0, 2 * SETS), :] = ahead(dst_ref[pl.ds(0, 2 * SETS), :], o)


def solve_angles(t_ref, offs_ref, step, cs_ref):
    _, turn, far = distances(offs_ref, step)
    d, e, a, b = [[t_ref[pl.ds(q * SETS + i, 1), :] for i in range(SETS)] for q in range(4)]
    for r in range(ROUNDS):
        gap = 0.5 * (d[0] - a[0])
        c0 = b[0]
        radius = jnp.sqrt(gap * gap + c0 * c0)
        sign = jnp.where(gap >= 0, 1.0, -1.0)
        t = -sign * c0 / (jnp.abs(gap) + radius + 1e-06 * (a[0] + d[0]))
        c = 1.0 / jnp.sqrt(1.0 + t * t)
        s = t * c
        cs_ref[pl.ds(r, 1), :] = c
        cs_ref[pl.ds(ROUNDS + r, 1), :] = s
        if r == ROUNDS - 1:
            break

        def partner(i):
            return (c, s) if i == 0 else (ahead(c, far[r][i]), ahead(s, far[r][i]))

        na, nb, nd, ne = [], [], [], []
        for i in KEPT[r][0]:
            cc, ss = partner(i)
            u1, u2 = cc * a[i] + ss * b[i], cc * e[i] + ss * d[i]
            v1, v2 = cc * b[i] - ss * a[i], cc * d[i] - ss * e[i]
            na.append(c * u1 + s * u2)
            nd.append(ahead(c * v2 - s * v1, turn[r]))
        for i in KEPT[r][1]:
            cc, ss = partner(i)
            v1, v2 = cc * b[i] - ss * a[i], cc * d[i] - ss * e[i]
            nb.append(c * v1 + s * v2)
        for i in KEPT[r][2]:
            if i is None:
                ne.append(nb[0])
                continue
            cc, ss = partner(i)
            u1, u2 = cc * a[i] + ss * b[i], cc * e[i] + ss * d[i]
            ne.append(ahead(c * u2 - s * u1, turn[r]))
        a, b, d, e = na, nb, nd, ne


def rotated(f, s, cs_ref, turn):
    shifts, back = turn
    for r in range(ROUNDS):
        s = pltpu.roll(s, shifts[r], 1)
        c = cs_ref[pl.ds(r, 1), :]
        n = cs_ref[pl.ds(ROUNDS + r, 1), :]
        f, s = f * c + s * n, s * c - f * n
    return f, pltpu.roll(s, back, 1)


def main_kernel(
    n_pair, n_row, rows, early, offs_hbm, x_hbm, x3f, x3s, w3f, w3s, cs_out, turn_out,
    offs_ref, x_in, xf, xs, of, os_, el, er, w_ref, gs, tot, cs, hl, hr, le, re,
    r0l, l0l, r0r, l0r, r1, l1, edge0, edge1,
    in_sem, g_send, g_recv, x_send, x_recv, e_send, e_recv, h_send, h_recv,
):
    k = lax.axis_index("pair")
    me = lax.axis_index("row")
    first, last = k == 0, k == n_pair - 1
    piece = rows // FETCHES
    late = []
    for n, sizes in zip(early, LATE):
        ends = [n + sum(sizes[: i + 1]) * (rows // 32) for i in range(len(sizes))]
        late.append([(end - size * (rows // 32), size * (rows // 32)) for end, size in zip(ends, sizes)])
    parts = [[(0, early[0])]] + [[(0, a)] + [(a, b - a)] * (b > a) for a, b in zip(early, early[1:])]

    fetch_offs = pltpu.make_async_copy(offs_hbm, offs_ref, in_sem.at[FETCHES])
    fetch_offs.start()
    fetch = [
        pltpu.make_async_copy(x_hbm.at[pl.ds(c * piece, piece)], x_in.at[pl.ds(c * piece, piece)], in_sem.at[c])
        for c in range(FETCHES)
    ]
    for copy in fetch:
        copy.start()

    barrier = pltpu.get_barrier_semaphore()

    @pl.when(k > 0)
    def _():
        pl.semaphore_signal(barrier, inc=1, device_id={"pair": k - 1}, device_id_type=MESH)

    @pl.when(k < n_pair - 1)
    def _():
        pl.semaphore_signal(barrier, inc=1, device_id={"pair": k + 1}, device_id_type=MESH)

    for j in range(1, n_row):
        pl.semaphore_signal(barrier, inc=1, device_id={"row": lax.rem(me + j, n_row)}, device_id_type=MESH)

    def to_right(src, dst, sems, at):
        return pltpu.make_async_remote_copy(
            src_ref=src, dst_ref=dst, send_sem=sems[0].at[(0,) + at], recv_sem=sems[1].at[(0,) + at],
            device_id={"pair": k + 1}, device_id_type=MESH,
        )

    def to_left(src, dst, sems, at):
        return pltpu.make_async_remote_copy(
            src_ref=src, dst_ref=dst, send_sem=sems[0].at[(1,) + at], recv_sem=sems[1].at[(1,) + at],
            device_id={"pair": k - 1}, device_id_type=MESH,
        )

    def arrived(dst_l, dst_r, sems, at):
        @pl.when(k > 0)
        def _():
            to_right(dst_l, dst_l, sems, at).wait_recv()

        @pl.when(k < n_pair - 1)
        def _():
            to_left(dst_r, dst_r, sems, at).wait_recv()

    def sent(src_r, src_l, sems, at):
        @pl.when(k < n_pair - 1)
        def _():
            to_right(src_r, src_r, sems, at).wait_send()

        @pl.when(k > 0)
        def _():
            to_left(src_l, src_l, sems, at).wait_send()

    def peer_copy(step, slot, to):
        return pltpu.make_async_remote_copy(
            src_ref=gs.at[step, slot], dst_ref=gs.at[step, slot], send_sem=g_send.at[step, to],
            recv_sem=g_recv.at[step, slot], device_id={"row": to}, device_id_type=MESH,
        )

    x_sems, e_sems, h_sems = (x_send, x_recv), (e_send, e_recv), (h_send, h_recv)

    def new(h, step):
        if step == STEPS - 2:
            return (x3f, x3s)[h]
        return (xf, xs)[h].at[step]

    def late_rows(step, c):
        return pl.ds(*late[step][c])

    def send_late(step, c):
        at = late_rows(step, c)
        f, s = of.at[step, at], os_.at[step, at]
        new_f, new_s = new(0, step).at[at], new(1, step).at[at]

        @pl.when(first)
        def _():
            to_right(s, new_f, x_sems, (step, c)).start()
            new_f[...] = f[...]

        @pl.when(jnp.logical_and(k > 0, k < n_pair - 1))
        def _():
            to_right(f, new_f, x_sems, (step, c)).start()

        @pl.when(last)
        def _():
            new_s[...] = f[...]

        @pl.when(k > 0)
        def _():
            to_left(s, new_s, x_sems, (step, c)).start()

    def early_moves(step, part):
        at = pl.ds(*parts[step][part])
        for h in range(2):
            if step == 0:
                src = x_in.at[at, pl.ds(h * B, B)]
                yield h, src, src, el.at[step, h, at], er.at[step, h, at]
            elif h == 0:
                yield h, new(0, step - 1).at[at], new(1, step - 1).at[at], el.at[step, 0, at], er.at[step, 1, at]

    def send_early(step, part):
        for h, to_r, to_l, from_l, from_r in early_moves(step, part):

            @pl.when(k < n_pair - 1)
            def _():
                to_right(to_r, from_l, e_sems, (step, h, part)).start()

            @pl.when(k > 0)
            def _():
                to_left(to_l, from_r, e_sems, (step, h, part)).start()

        at = pl.ds(*parts[step][part])
        own = [x_in.at[at, pl.ds(h * B, B)] if step == 0 else new(h, step - 1).at[at] for h in range(2)]

        @pl.when(first)
        def _():
            for h in range(2):
                el[step, h, at] = own[h][...]

        @pl.when(last)
        def _():
            for h in range(2):
                er[step, h, at] = own[h][...]

    def rotate_own_early(step):
        top = pl.ds(0, early[step])
        if step == 0:
            f, s = x_in[top, :B], x_in[top, B:]
        else:
            f, s = xf[step - 1, top, :], xs[step - 1, top, :]
        of[step, top, :], os_[step, top, :] = rotated(f, s, cs.at[step], turns(offs_ref, step))

    def rotate_early(step):
        top = pl.ds(0, early[step])
        for part in range(len(parts[step])):
            for h, _, _, from_l, from_r in early_moves(step, part):
                arrived(from_l, from_r, e_sems, (step, h, part))
        turn = turns(offs_ref, step)
        f, s = el[step, 0, top], el[step, 1, top]
        if step > 0:
            s = jnp.where(first, s, os_[step - 1, top, :])
        f, s = rotated(f, s, hl.at[step, step], turn)
        new(0, step)[top, :] = jnp.where(k == 1, s, f)
        f, s = er[step, 0, top], er[step, 1, top]
        if step > 0:
            f = jnp.where(last, f, jnp.where(first, os_[step - 1, top, :], of[step - 1, top, :]))
        f, s = rotated(f, s, hr.at[step, step], turn)
        new(1, step)[top, :] = jnp.where(last, f, s)

    def send_history(step):
        if step > 0:
            le[step, pl.ds(0, step)] = hl[step - 1, pl.ds(0, step)]
            re[step, pl.ds(0, step)] = hr[step - 1, pl.ds(0, step)]
        le[step, step] = cs[step]
        re[step, step] = cs[step]
        n = pl.ds(0, step + 1)

        @pl.when(k < n_pair - 1)
        def _():
            to_right(le.at[step, n], hl.at[step, n], h_sems, (step,)).start()

        @pl.when(k > 0)
        def _():
            to_left(re.at[step, n], hr.at[step, n], h_sems, (step,)).start()

        @pl.when(first)
        def _():
            hl[step, n] = re[step, n]

        @pl.when(last)
        def _():
            hr[step, n] = le[step, n]

    def node(level, slot, cs_ref, from_left, from_right, dst_right, dst_left):
        turn = turns(offs_ref, level)
        outside = jnp.logical_or(slot < 0, slot >= n_pair)
        swap = jnp.logical_or(jnp.logical_or(slot < -1, slot == 0), slot >= n_pair)
        if level == 0:
            row = lax.broadcasted_iota(jnp.int32, (WIDTH, B), 0)
            col = lax.broadcasted_iota(jnp.int32, (WIDTH, B), 1)
            f, s = [jnp.where(row == col + h, 1.0, 0.0).astype(F32) for h in (0, B)]
        else:
            zero = jnp.zeros((WIDTH, B), F32)
            p = jnp.concatenate([from_left[...], zero], axis=0)
            q = jnp.concatenate([zero, from_right[...]], axis=0)
            f, s = jnp.where(outside, q, p), jnp.where(outside, p, q)
        f, s = rotated(f, s, cs_ref, turn)
        if dst_right is not None:
            dst_right[...] = jnp.where(swap, s, f)
        if dst_left is not None:
            dst_left[...] = jnp.where(swap, f, s)

    def rebuild(step):
        if step == 1:
            node(0, k - 1, hl.at[0, 0], None, None, r0l, l0l)
            node(0, k + 1, hr.at[0, 0], None, None, r0r, l0r)
        if step == 2:
            node(1, k, cs.at[1], r0l, l0r, r1, l1)
        if step == 3:
            node(0, k - 3, hl.at[2, 0], None, None, edge0.at[0], None)
            node(0, k + 3, hr.at[2, 0], None, None, None, edge0.at[1])
            node(1, k - 2, hl.at[2, 1], edge0.at[0], l0l, edge1.at[0], None)
            node(1, k + 2, hr.at[2, 1], r0r, edge0.at[1], None, edge1.at[1])
            node(2, k - 1, hl.at[2, 2], edge1.at[0], l1, w3f, None)
            node(2, k + 1, hr.at[2, 2], r1, edge1.at[1], None, w3s)

    total = jnp.zeros((WIDTH, WIDTH), F32)
    for c in range(FETCHES // 2):
        fetch[c].wait()
        total = total + gram(x_in[pl.ds(c * piece, piece), :])
    pl.semaphore_wait(barrier, n_row - 1 + (k > 0).astype(jnp.int32) + (k < n_pair - 1).astype(jnp.int32))
    send_early(0, 0)
    for c in range(FETCHES // 2, FETCHES):
        fetch[c].wait()
        total = total + gram(x_in[pl.ds(c * piece, piece), :])
    fetch_offs.wait()
    for step in range(STEPS):
        pick_diagonals(total, w_ref, gs.at[step, me], offs_ref, step)
        for j in range(1, n_row):
            peer_copy(step, me, lax.rem(me + j, n_row)).start()
        if 0 < step < STEPS - 1:
            rotate_own_early(step - 1)
        rebuild(step)
        for j in range(1, n_row):
            peer_copy(step, lax.rem(me + j, n_row), lax.rem(me + j, n_row)).wait_recv()
        tot[...] = sum((gs[step, i] for i in range(1, n_row)), gs[step, 0])
        solve_angles(tot, offs_ref, step, cs.at[step])
        if step == STEPS - 1:
            break
        turn = turns(offs_ref, step)
        send_history(step)
        for c in range(len(late[step])):
            at = late_rows(step, c)
            if step == 0:
                f, s = x_in[at, :B], x_in[at, B:]
            else:
                f, s = xf[step - 1, at, :], xs[step - 1, at, :]
            f, s = rotated(f, s, cs.at[step], turn)
            of[step, at, :] = f
            os_[step, at, :] = s
            send_late(step, c)
        n = pl.ds(0, step + 1)
        arrived(hl.at[step, n], hr.at[step, n], h_sems, (step,))
        rotate_early(step)
        if step + 1 < STEPS - 1:
            send_early(step + 1, 0)
        top = pl.ds(0, early[step])
        total = gram(jnp.concatenate([new(h, step)[top, :] for h in range(2)], axis=1))
        for c in range(len(late[step])):
            at = late_rows(step, c)
            arrived(new(0, step).at[at], new(1, step).at[at], x_sems, (step, c))
            if step + 1 < STEPS - 1 and len(parts[step + 1]) > 1 and sum(late[step][c]) == early[step + 1]:
                send_early(step + 1, 1)
            total = total + gram(jnp.concatenate([new(h, step)[at, :] for h in range(2)], axis=1))

    cs_out[...] = cs[STEPS - 1]
    shifts, back = turns(offs_ref, STEPS - 1)
    row = lax.broadcasted_iota(jnp.int32, (2 * ROUNDS, B), 0)
    table = jnp.full((2 * ROUNDS, B), back, jnp.int32)
    for r in range(ROUNDS):
        table = jnp.where(row == r, shifts[r], table)
    turn_out[...] = table

    for step in range(STEPS):
        for j in range(1, n_row):
            peer_copy(step, me, lax.rem(me + j, n_row)).wait_send()
        if step < STEPS - 1:
            n = pl.ds(0, step + 1)
            sent(le.at[step, n], re.at[step, n], h_sems, (step,))
            for part in range(len(parts[step])):
                for h, to_r, to_l, _, _ in early_moves(step, part):
                    sent(to_r, to_l, e_sems, (step, h, part))
            for c in range(len(late[step])):
                at = late_rows(step, c)
                sent(of.at[step, at], os_.at[step, at], x_sems, (step, c))


def place_kernel(n_pair, blocks, turn_ref, cs_ref, xf, xs, wf, ws, x_out, v_out, x_last, w_last, zero, sem):
    k, me = lax.axis_index("pair"), lax.axis_index("row")
    half = xf.shape[0] // 2
    zero[...] = jnp.zeros_like(zero)
    slots = []
    for j in range(STEPS):
        slot = k - (STEPS - 1) + 2 * j
        slot = jnp.where(slot < 0, -1 - slot, slot)
        slots.append(jnp.where(slot >= n_pair, 2 * n_pair - 1 - slot, slot) - me * blocks)

    def piece(j):
        here = jnp.logical_and(slots[j] >= 0, slots[j] < blocks)
        place = pl.multiple_of(jnp.where(here, slots[j], 0) * WIDTH, WIDTH)
        return here, pltpu.make_async_copy(
            w_last.at[pl.ds(j * WIDTH, WIDTH)], v_out.at[pl.ds(place, WIDTH)], sem.at[blocks + j]
        )

    def blank(b):
        empty = slots[0] != b
        for j in range(1, STEPS):
            empty = jnp.logical_and(empty, slots[j] != b)
        return empty, pltpu.make_async_copy(zero, v_out.at[pl.ds(b * WIDTH, WIDTH)], sem.at[b])

    pieces, blanks = [piece(j) for j in range(STEPS)], [blank(b) for b in range(blocks)]
    for needed, copy in blanks:
        pl.when(needed)(copy.start)
    turn = [turn_ref[r, 0] for r in range(ROUNDS)], turn_ref[ROUNDS, 0]
    moves = []
    for g in range(2):
        at = pl.ds(g * half, half)
        f, s = rotated(xf[at, :], xs[at, :], cs_ref, turn)
        x_last[at, :B] = f
        x_last[at, B:] = s
        moves.append(pltpu.make_async_copy(x_last.at[at], x_out.at[at], sem.at[blocks + STEPS + g]))
        moves[-1].start()
    blank_rows = jnp.zeros((WIDTH, B), F32)
    parts = [
        (wf[: 2 * WIDTH, :], jnp.concatenate([blank_rows, ws[:WIDTH, :]], axis=0)),
        (jnp.concatenate([wf[2 * WIDTH :, :], blank_rows], axis=0), ws[WIDTH:, :]),
    ]
    for g, (f, s) in enumerate(parts):
        at = pl.ds(g * 2 * WIDTH, 2 * WIDTH)
        f, s = rotated(f, s, cs_ref, turn)
        w_last[at, :B] = f
        w_last[at, B:] = s
        for needed, copy in pieces[2 * g : 2 * g + 2]:
            pl.when(needed)(copy.start)
    for needed, copy in pieces + blanks:
        pl.when(needed)(copy.wait)
    for copy in moves:
        copy.wait()


def body(n_pair, n_row, whitened, offsets):
    rows, width = whitened.shape
    v_rows = n_pair * width // n_row
    blocks = v_rows // width
    early = [rows * n // 16 for n in EARLY]
    sds = functools.partial(jax.ShapeDtypeStruct, dtype=F32)
    vmem = pl.BlockSpec(memory_space=pltpu.VMEM)
    anywhere = pl.BlockSpec(memory_space=pl.ANY)
    hbm = pl.BlockSpec(memory_space=pltpu.HBM)
    dma = pltpu.SemaphoreType.DMA

    def held(*shape):
        return pltpu.VMEM(shape, F32)

    *held_rows, cs, turn = pl.pallas_call(
        functools.partial(main_kernel, n_pair, n_row, rows, early),
        out_shape=[sds((rows, B))] * 2
        + [sds(((STEPS - 1) * width, B))] * 2
        + [sds((2 * ROUNDS, B)), jax.ShapeDtypeStruct((2 * ROUNDS, B), jnp.int32)],
        in_specs=[hbm, hbm],
        out_specs=[vmem] * 6,
        scratch_shapes=[
            pltpu.SMEM((STEPS, ROUNDS), jnp.int32),
            held(rows, width),
            held(STEPS - 2, rows, B),
            held(STEPS - 2, rows, B),
            held(STEPS - 1, rows, B),
            held(STEPS - 1, rows, B),
            held(STEPS - 1, 2, max(early), B),
            held(STEPS - 1, 2, max(early), B),
            held(4, B, B),
            held(STEPS, n_row, ROWS_SENT, B),
            held(ROWS_SENT, B),
            held(STEPS, 2 * ROUNDS, B),
        ]
        + [held(STEPS - 1, STEPS - 1, 2 * ROUNDS, B) for _ in range(4)]
        + [held(n * width, B) for n in (1, 1, 1, 1, 2, 2)]
        + [held(2, width, B), held(2, 2 * width, B)]
        + [
            dma((FETCHES + 1,)),
            dma((STEPS, n_row)),
            dma((STEPS, n_row)),
            dma((2, STEPS - 1, max(map(len, LATE)))),
            dma((2, STEPS - 1, max(map(len, LATE)))),
            dma((2, STEPS - 1, 2, 2)),
            dma((2, STEPS - 1, 2, 2)),
            dma((2, STEPS - 1)),
            dma((2, STEPS - 1)),
        ],
        compiler_params=pltpu.CompilerParams(
            collective_id=0, has_side_effects=True, vmem_limit_bytes=40 * 1024 * 1024
        ),
    )(pltpu.with_memory_space_constraint(offsets, pltpu.HBM), pltpu.with_memory_space_constraint(whitened, pltpu.HBM))
    return pl.pallas_call(
        functools.partial(place_kernel, n_pair, blocks),
        out_shape=[sds((rows, width)), sds((v_rows, width))],
        in_specs=[vmem] * 6,
        out_specs=[anywhere, anywhere],
        scratch_shapes=[held(rows, width), held(STEPS * width, width), held(width, width), dma((blocks + STEPS + 2,))],
        compiler_params=pltpu.CompilerParams(vmem_limit_bytes=8 * 1024 * 1024),
    )(turn, cs, *held_rows)


def solution(mesh):
    n_pair, n_row = mesh.shape["pair"], mesh.shape["row"]
    return jax.shard_map(
        functools.partial(body, n_pair, n_row),
        mesh=mesh,
        in_specs=(P("row", "pair"), P()),
        out_specs=(P("row", "pair"), P("row", "pair")),
        check_vma=False,
    )
```

```python
import functools

import jax
import jax.numpy as jnp
from jax import lax
from jax.experimental import pallas as pl
from jax.experimental.pallas import tpu as pltpu
from jax.sharding import PartitionSpec as P

B = 128
WIDTH = 2 * B
ROUNDS = 4
STEPS = 4
FETCHES = 4
EARLY = (7, 12, 12)
TILES = (2, 3, 3)
LATE = ((4, 6, 4, 4), (6, 2), (6, 2))
SETS = 14
ROWS_SENT = 4 * SETS
MESH = pl.DeviceIdType.MESH
F32 = jnp.float32

KEPT = [
    ([0, 1, 2, 3, 4], [5, 6, 7, 8, 9], [None, 10, 11, 12, 13]),
    ([0, 2], [1, 3], [None, 4]),
    ([0], [1], [None]),
]


def gram(x):
    return lax.dot_general(x, x, (((0,), (0,)), ((), ())), precision=lax.Precision.HIGHEST, preferred_element_type=F32)


def ahead(x, by):
    return pltpu.roll(x, lax.rem(B - by, B), 1)


def turns(offs_ref, step):
    offs = [offs_ref[step, r] for r in range(ROUNDS)]
    before = [jnp.int32(0)] + offs[:-1]
    return [lax.rem(b - o + B, B) for b, o in zip(before, offs)], offs[-1]


def distances(offs_ref, step):
    o = [offs_ref[step, r] for r in range(ROUNDS)]
    d1, d2, d3 = [lax.rem(b - a + B, B) for a, b in zip(o, o[1:])]
    near = [jnp.int32(0), d2, d3, d3 + d2, d3 - d2]
    far = near + [e + d1 for e in near] + [e - d1 for e in near[1:]]
    far = [lax.rem(e + 2 * B, B) for e in far]
    return o[0], (d1, d2, d3), [far, far[:5], [far[0], far[2]]]


def pick_diagonals(total, w_ref, dst_ref, offs_ref, step):
    o, _, far = distances(offs_ref, step)
    w_ref[0] = total[B:, B:]
    w_ref[1] = total[:B, B:]
    w_ref[2] = total[:B, :B]
    w_ref[3] = total[B:, :B]
    base = lax.broadcasted_iota(jnp.int32, (8, B), 0) - lax.broadcasted_iota(jnp.int32, (8, B), 1)
    same, to_first, to_second = far[0], [lax.rem(e - o + B, B) for e in far[0]], [lax.rem(e + o, B) for e in far[0]]
    for at, blocks in ((same, (0, 2)), (to_first, (1,)), (to_second, (3,))):
        acc = [[jnp.zeros((8, B), F32) for _ in at] for _ in blocks]
        for g in range(B // 8):
            dist = (base + 8 * g) & (B - 1)
            m = [w_ref[q, 8 * g : 8 * g + 8, :] for q in blocks]
            for i, t in enumerate(at):
                here = dist == t
                for n in range(len(blocks)):
                    acc[n][i] = jnp.where(here, m[n], acc[n][i])
        for n, q in enumerate(blocks):
            for i, v in enumerate(acc[n]):
                dst_ref[pl.ds(q * SETS + i, 1), :] = jnp.sum(v, axis=0, keepdims=True)
    dst_ref[pl.ds(0, 2 * SETS), :] = ahead(dst_ref[pl.ds(0, 2 * SETS), :], o)


def solve_angles(t_ref, offs_ref, step, cs_ref):
    _, turn, far = distances(offs_ref, step)
    d, e, a, b = [[t_ref[pl.ds(q * SETS + i, 1), :] for i in range(SETS)] for q in range(4)]
    for r in range(ROUNDS):
        gap = 0.5 * (d[0] - a[0])
        c0 = b[0]
        radius = jnp.sqrt(gap * gap + c0 * c0)
        sign = jnp.where(gap >= 0, 1.0, -1.0)
        t = -sign * c0 / (jnp.abs(gap) + radius + 1e-06 * (a[0] + d[0]))
        c = 1.0 / jnp.sqrt(1.0 + t * t)
        s = t * c
        cs_ref[pl.ds(r, 1), :] = c
        cs_ref[pl.ds(ROUNDS + r, 1), :] = s
        if r == ROUNDS - 1:
            break

        def partner(i):
            return (c, s) if i == 0 else (ahead(c, far[r][i]), ahead(s, far[r][i]))

        na, nb, nd, ne = [], [], [], []
        for i in KEPT[r][0]:
            cc, ss = partner(i)
            u1, u2 = cc * a[i] + ss * b[i], cc * e[i] + ss * d[i]
            v1, v2 = cc * b[i] - ss * a[i], cc * d[i] - ss * e[i]
            na.append(c * u1 + s * u2)
            nd.append(ahead(c * v2 - s * v1, turn[r]))
        for i in KEPT[r][1]:
            cc, ss = partner(i)
            v1, v2 = cc * b[i] - ss * a[i], cc * d[i] - ss * e[i]
            nb.append(c * v1 + s * v2)
        for i in KEPT[r][2]:
            if i is None:
                ne.append(nb[0])
                continue
            cc, ss = partner(i)
            u1, u2 = cc * a[i] + ss * b[i], cc * e[i] + ss * d[i]
            ne.append(ahead(c * u2 - s * u1, turn[r]))
        a, b, d, e = na, nb, nd, ne


def rotated(f, s, cs_ref, turn):
    shifts, back = turn
    for r in range(ROUNDS):
        s = pltpu.roll(s, shifts[r], 1)
        c = cs_ref[pl.ds(r, 1), :]
        n = cs_ref[pl.ds(ROUNDS + r, 1), :]
        f, s = f * c + s * n, s * c - f * n
    return f, pltpu.roll(s, back, 1)


def main_kernel(
    n_pair, n_row, rows, early, offs_hbm, x_hbm, x3f, x3s, w3f, w3s, cs_out, turn_out,
    offs_ref, x_in, xf, xs, of, os_, el, er, w_ref, gs, tot, cs, hl, hr, le, re,
    r0l, l0l, r0r, l0r, r1, l1, edge0, edge1,
    in_sem, g_send, g_recv, x_send, x_recv, e_send, e_recv, h_send, h_recv,
):
    k = lax.axis_index("pair")
    me = lax.axis_index("row")
    first, last = k == 0, k == n_pair - 1
    piece = rows // FETCHES
    late = []
    for n, sizes in zip(early, LATE):
        ends = [n + sum(sizes[: i + 1]) * (rows // 32) for i in range(len(sizes))]
        late.append([(end - size * (rows // 32), size * (rows // 32)) for end, size in zip(ends, sizes)])
    parts = [[(0, early[0])]] + [[(0, a)] + [(a, b - a)] * (b > a) for a, b in zip(early, early[1:])]

    fetch_offs = pltpu.make_async_copy(offs_hbm, offs_ref, in_sem.at[FETCHES])
    fetch_offs.start()
    fetch = [
        pltpu.make_async_copy(x_hbm.at[pl.ds(c * piece, piece)], x_in.at[pl.ds(c * piece, piece)], in_sem.at[c])
        for c in range(FETCHES)
    ]
    for copy in fetch:
        copy.start()

    barrier = pltpu.get_barrier_semaphore()

    @pl.when(k > 0)
    def _():
        pl.semaphore_signal(barrier, inc=1, device_id={"pair": k - 1}, device_id_type=MESH)

    @pl.when(k < n_pair - 1)
    def _():
        pl.semaphore_signal(barrier, inc=1, device_id={"pair": k + 1}, device_id_type=MESH)

    for j in range(1, n_row):
        pl.semaphore_signal(barrier, inc=1, device_id={"row": lax.rem(me + j, n_row)}, device_id_type=MESH)

    def to_right(src, dst, sems, at):
        return pltpu.make_async_remote_copy(
            src_ref=src, dst_ref=dst, send_sem=sems[0].at[(0,) + at], recv_sem=sems[1].at[(0,) + at],
            device_id={"pair": k + 1}, device_id_type=MESH,
        )

    def to_left(src, dst, sems, at):
        return pltpu.make_async_remote_copy(
            src_ref=src, dst_ref=dst, send_sem=sems[0].at[(1,) + at], recv_sem=sems[1].at[(1,) + at],
            device_id={"pair": k - 1}, device_id_type=MESH,
        )

    def arrived(dst_l, dst_r, sems, at):
        @pl.when(k > 0)
        def _():
            to_right(dst_l, dst_l, sems, at).wait_recv()

        @pl.when(k < n_pair - 1)
        def _():
            to_left(dst_r, dst_r, sems, at).wait_recv()

    def sent(src_r, src_l, sems, at):
        @pl.when(k < n_pair - 1)
        def _():
            to_right(src_r, src_r, sems, at).wait_send()

        @pl.when(k > 0)
        def _():
            to_left(src_l, src_l, sems, at).wait_send()

    def peer_copy(step, slot, to):
        return pltpu.make_async_remote_copy(
            src_ref=gs.at[step, slot], dst_ref=gs.at[step, slot], send_sem=g_send.at[step, to],
            recv_sem=g_recv.at[step, slot], device_id={"row": to}, device_id_type=MESH,
        )

    x_sems, e_sems, h_sems = (x_send, x_recv), (e_send, e_recv), (h_send, h_recv)

    def new(h, step):
        if step == STEPS - 2:
            return (x3f, x3s)[h]
        return (xf, xs)[h].at[step]

    def late_rows(step, c):
        return pl.ds(*late[step][c])

    def send_late(step, c):
        at = late_rows(step, c)
        f, s = of.at[step, at], os_.at[step, at]
        new_f, new_s = new(0, step).at[at], new(1, step).at[at]

        @pl.when(first)
        def _():
            to_right(s, new_f, x_sems, (step, c)).start()
            new_f[...] = f[...]

        @pl.when(jnp.logical_and(k > 0, k < n_pair - 1))
        def _():
            to_right(f, new_f, x_sems, (step, c)).start()

        @pl.when(last)
        def _():
            new_s[...] = f[...]

        @pl.when(k > 0)
        def _():
            to_left(s, new_s, x_sems, (step, c)).start()

    def early_moves(step, part):
        at = pl.ds(*parts[step][part])
        for h in range(2):
            if step == 0:
                src = x_in.at[at, pl.ds(h * B, B)]
                yield h, src, src, el.at[step, h, at], er.at[step, h, at]
            elif h == 0:
                yield h, new(0, step - 1).at[at], new(1, step - 1).at[at], el.at[step, 0, at], er.at[step, 1, at]

    def send_early(step, part):
        for h, to_r, to_l, from_l, from_r in early_moves(step, part):

            @pl.when(k < n_pair - 1)
            def _():
                to_right(to_r, from_l, e_sems, (step, h, part)).start()

            @pl.when(k > 0)
            def _():
                to_left(to_l, from_r, e_sems, (step, h, part)).start()

    def keep_own(step):
        top = pl.ds(0, early[step])
        own = [x_in.at[top, pl.ds(h * B, B)] if step == 0 else new(h, step - 1).at[top] for h in range(2)]

        @pl.when(first)
        def _():
            for h in range(2):
                el[step, h, top] = own[h][...]

        @pl.when(last)
        def _():
            for h in range(2):
                er[step, h, top] = own[h][...]

    def hold(step, at, f, s):
        el[step + 1, 1, at] = s
        er[step + 1, 0, at] = jnp.where(first, s, f)

    def rotate_own_early(step):
        top = pl.ds(0, early[step])
        if step == 0:
            f, s = x_in[top, :B], x_in[top, B:]
        else:
            f, s = xf[step - 1, top, :], xs[step - 1, top, :]
        f, s = rotated(f, s, cs.at[step], turns(offs_ref, step))
        hold(step, top, f, s)

    def early_gram(step):
        for part in range(len(parts[step])):
            for h, _, _, from_l, from_r in early_moves(step, part):
                arrived(from_l, from_r, e_sems, (step, h, part))
        turn = turns(offs_ref, step)
        tile = early[step] // TILES[step]
        total = jnp.zeros((WIDTH, WIDTH), F32)
        for c in range(TILES[step]):
            at = pl.ds(c * tile, tile)
            f, s = rotated(el[step, 0, at], el[step, 1, at], hl.at[step, step], turn)
            new_f = jnp.where(k == 1, s, f)
            f, s = rotated(er[step, 0, at], er[step, 1, at], hr.at[step, step], turn)
            new_s = jnp.where(last, f, s)
            new(0, step)[at, :] = new_f
            new(1, step)[at, :] = new_s
            total = total + gram(jnp.concatenate([new_f, new_s], axis=1))
        return total

    def send_history(step):
        if step > 0:
            le[step, pl.ds(0, step)] = hl[step - 1, pl.ds(0, step)]
            re[step, pl.ds(0, step)] = hr[step - 1, pl.ds(0, step)]
        le[step, step] = cs[step]
        re[step, step] = cs[step]
        n = pl.ds(0, step + 1)

        @pl.when(k < n_pair - 1)
        def _():
            to_right(le.at[step, n], hl.at[step, n], h_sems, (step,)).start()

        @pl.when(k > 0)
        def _():
            to_left(re.at[step, n], hr.at[step, n], h_sems, (step,)).start()

        @pl.when(first)
        def _():
            hl[step, n] = re[step, n]

        @pl.when(last)
        def _():
            hr[step, n] = le[step, n]

    def node(level, slot, cs_ref, from_left, from_right, dst_right, dst_left):
        turn = turns(offs_ref, level)
        outside = jnp.logical_or(slot < 0, slot >= n_pair)
        swap = jnp.logical_or(jnp.logical_or(slot < -1, slot == 0), slot >= n_pair)
        if level == 0:
            row = lax.broadcasted_iota(jnp.int32, (WIDTH, B), 0)
            col = lax.broadcasted_iota(jnp.int32, (WIDTH, B), 1)
            f, s = [jnp.where(row == col + h, 1.0, 0.0).astype(F32) for h in (0, B)]
        else:
            zero = jnp.zeros((WIDTH, B), F32)
            p = jnp.concatenate([from_left[...], zero], axis=0)
            q = jnp.concatenate([zero, from_right[...]], axis=0)
            f, s = jnp.where(outside, q, p), jnp.where(outside, p, q)
        f, s = rotated(f, s, cs_ref, turn)
        if dst_right is not None:
            dst_right[...] = jnp.where(swap, s, f)
        if dst_left is not None:
            dst_left[...] = jnp.where(swap, f, s)

    def rebuild(step):
        if step == 1:
            node(0, k - 1, hl.at[0, 0], None, None, r0l, l0l)
            node(0, k + 1, hr.at[0, 0], None, None, r0r, l0r)
        if step == 2:
            node(1, k, cs.at[1], r0l, l0r, r1, l1)
        if step == 3:
            node(0, k - 3, hl.at[2, 0], None, None, edge0.at[0], None)
            node(0, k + 3, hr.at[2, 0], None, None, None, edge0.at[1])
            node(1, k - 2, hl.at[2, 1], edge0.at[0], l0l, edge1.at[0], None)
            node(1, k + 2, hr.at[2, 1], r0r, edge0.at[1], None, edge1.at[1])
            node(2, k - 1, hl.at[2, 2], edge1.at[0], l1, w3f, None)
            node(2, k + 1, hr.at[2, 2], r1, edge1.at[1], None, w3s)

    total = jnp.zeros((WIDTH, WIDTH), F32)
    for c in range(FETCHES // 2):
        fetch[c].wait()
        total = total + gram(x_in[pl.ds(c * piece, piece), :])
    pl.semaphore_wait(barrier, n_row - 1 + (k > 0).astype(jnp.int32) + (k < n_pair - 1).astype(jnp.int32))
    send_early(0, 0)
    keep_own(0)
    for c in range(FETCHES // 2, FETCHES):
        fetch[c].wait()
        total = total + gram(x_in[pl.ds(c * piece, piece), :])
    fetch_offs.wait()
    for step in range(STEPS):
        pick_diagonals(total, w_ref, gs.at[step, me], offs_ref, step)
        for j in range(1, n_row):
            peer_copy(step, me, lax.rem(me + j, n_row)).start()
        if 0 < step < STEPS - 1:
            rotate_own_early(step - 1)
            keep_own(step)
        rebuild(step)
        for j in range(1, n_row):
            peer_copy(step, lax.rem(me + j, n_row), lax.rem(me + j, n_row)).wait_recv()
        tot[...] = sum((gs[step, i] for i in range(1, n_row)), gs[step, 0])
        solve_angles(tot, offs_ref, step, cs.at[step])
        if step == STEPS - 1:
            break
        turn = turns(offs_ref, step)
        send_history(step)
        for c in range(len(late[step])):
            at = late_rows(step, c)
            if step == 0:
                f, s = x_in[at, :B], x_in[at, B:]
            else:
                f, s = xf[step - 1, at, :], xs[step - 1, at, :]
            f, s = rotated(f, s, cs.at[step], turn)
            of[step, at, :] = f
            os_[step, at, :] = s
            send_late(step, c)
            if step + 1 < STEPS - 1 and sum(late[step][c]) <= early[step + 1]:
                hold(step, at, f, s)
        n = pl.ds(0, step + 1)
        arrived(hl.at[step, n], hr.at[step, n], h_sems, (step,))
        total = early_gram(step)
        if step + 1 < STEPS - 1:
            send_early(step + 1, 0)
        for c in range(len(late[step])):
            at = late_rows(step, c)
            arrived(new(0, step).at[at], new(1, step).at[at], x_sems, (step, c))
            if step + 1 < STEPS - 1 and len(parts[step + 1]) > 1 and sum(late[step][c]) == early[step + 1]:
                send_early(step + 1, 1)
            total = total + gram(jnp.concatenate([new(h, step)[at, :] for h in range(2)], axis=1))

    cs_out[...] = cs[STEPS - 1]
    shifts, back = turns(offs_ref, STEPS - 1)
    row = lax.broadcasted_iota(jnp.int32, (2 * ROUNDS, B), 0)
    table = jnp.full((2 * ROUNDS, B), back, jnp.int32)
    for r in range(ROUNDS):
        table = jnp.where(row == r, shifts[r], table)
    turn_out[...] = table

    for step in range(STEPS):
        for j in range(1, n_row):
            peer_copy(step, me, lax.rem(me + j, n_row)).wait_send()
        if step < STEPS - 1:
            n = pl.ds(0, step + 1)
            sent(le.at[step, n], re.at[step, n], h_sems, (step,))
            for part in range(len(parts[step])):
                for h, to_r, to_l, _, _ in early_moves(step, part):
                    sent(to_r, to_l, e_sems, (step, h, part))
            for c in range(len(late[step])):
                at = late_rows(step, c)
                sent(of.at[step, at], os_.at[step, at], x_sems, (step, c))


def place_kernel(n_pair, blocks, turn_ref, cs_ref, xf, xs, wf, ws, x_out, v_out, x_last, w_last, zero, sem):
    k, me = lax.axis_index("pair"), lax.axis_index("row")
    half = xf.shape[0] // 2
    zero[...] = jnp.zeros_like(zero)
    slots = []
    for j in range(STEPS):
        slot = k - (STEPS - 1) + 2 * j
        slot = jnp.where(slot < 0, -1 - slot, slot)
        slots.append(jnp.where(slot >= n_pair, 2 * n_pair - 1 - slot, slot) - me * blocks)

    def piece(j):
        here = jnp.logical_and(slots[j] >= 0, slots[j] < blocks)
        place = pl.multiple_of(jnp.where(here, slots[j], 0) * WIDTH, WIDTH)
        return here, pltpu.make_async_copy(
            w_last.at[pl.ds(j * WIDTH, WIDTH)], v_out.at[pl.ds(place, WIDTH)], sem.at[blocks + j]
        )

    def blank(b):
        empty = slots[0] != b
        for j in range(1, STEPS):
            empty = jnp.logical_and(empty, slots[j] != b)
        return empty, pltpu.make_async_copy(zero, v_out.at[pl.ds(b * WIDTH, WIDTH)], sem.at[b])

    pieces, blanks = [piece(j) for j in range(STEPS)], [blank(b) for b in range(blocks)]
    for needed, copy in blanks:
        pl.when(needed)(copy.start)
    turn = [turn_ref[r, 0] for r in range(ROUNDS)], turn_ref[ROUNDS, 0]
    moves = []
    for g in range(2):
        at = pl.ds(g * half, half)
        f, s = rotated(xf[at, :], xs[at, :], cs_ref, turn)
        x_last[at, :B] = f
        x_last[at, B:] = s
        moves.append(pltpu.make_async_copy(x_last.at[at], x_out.at[at], sem.at[blocks + STEPS + g]))
        moves[-1].start()
    blank_rows = jnp.zeros((WIDTH, B), F32)
    parts = [
        (wf[: 2 * WIDTH, :], jnp.concatenate([blank_rows, ws[:WIDTH, :]], axis=0)),
        (jnp.concatenate([wf[2 * WIDTH :, :], blank_rows], axis=0), ws[WIDTH:, :]),
    ]
    for g, (f, s) in enumerate(parts):
        at = pl.ds(g * 2 * WIDTH, 2 * WIDTH)
        f, s = rotated(f, s, cs_ref, turn)
        w_last[at, :B] = f
        w_last[at, B:] = s
        for needed, copy in pieces[2 * g : 2 * g + 2]:
            pl.when(needed)(copy.start)
    for needed, copy in pieces + blanks:
        pl.when(needed)(copy.wait)
    for copy in moves:
        copy.wait()


def body(n_pair, n_row, whitened, offsets):
    rows, width = whitened.shape
    v_rows = n_pair * width // n_row
    blocks = v_rows // width
    early = [rows * n // 16 for n in EARLY]
    sds = functools.partial(jax.ShapeDtypeStruct, dtype=F32)
    vmem = pl.BlockSpec(memory_space=pltpu.VMEM)
    anywhere = pl.BlockSpec(memory_space=pl.ANY)
    hbm = pl.BlockSpec(memory_space=pltpu.HBM)
    dma = pltpu.SemaphoreType.DMA

    def held(*shape):
        return pltpu.VMEM(shape, F32)

    *held_rows, cs, turn = pl.pallas_call(
        functools.partial(main_kernel, n_pair, n_row, rows, early),
        out_shape=[sds((rows, B))] * 2
        + [sds(((STEPS - 1) * width, B))] * 2
        + [sds((2 * ROUNDS, B)), jax.ShapeDtypeStruct((2 * ROUNDS, B), jnp.int32)],
        in_specs=[hbm, hbm],
        out_specs=[vmem] * 6,
        scratch_shapes=[
            pltpu.SMEM((STEPS, ROUNDS), jnp.int32),
            held(rows, width),
            held(STEPS - 2, rows, B),
            held(STEPS - 2, rows, B),
            held(STEPS - 1, rows, B),
            held(STEPS - 1, rows, B),
            held(STEPS - 1, 2, max(early), B),
            held(STEPS - 1, 2, max(early), B),
            held(4, B, B),
            held(STEPS, n_row, ROWS_SENT, B),
            held(ROWS_SENT, B),
            held(STEPS, 2 * ROUNDS, B),
        ]
        + [held(STEPS - 1, STEPS - 1, 2 * ROUNDS, B) for _ in range(4)]
        + [held(n * width, B) for n in (1, 1, 1, 1, 2, 2)]
        + [held(2, width, B), held(2, 2 * width, B)]
        + [
            dma((FETCHES + 1,)),
            dma((STEPS, n_row)),
            dma((STEPS, n_row)),
            dma((2, STEPS - 1, max(map(len, LATE)))),
            dma((2, STEPS - 1, max(map(len, LATE)))),
            dma((2, STEPS - 1, 2, 2)),
            dma((2, STEPS - 1, 2, 2)),
            dma((2, STEPS - 1)),
            dma((2, STEPS - 1)),
        ],
        compiler_params=pltpu.CompilerParams(
            collective_id=0, has_side_effects=True, vmem_limit_bytes=40 * 1024 * 1024
        ),
    )(pltpu.with_memory_space_constraint(offsets, pltpu.HBM), pltpu.with_memory_space_constraint(whitened, pltpu.HBM))
    return pl.pallas_call(
        functools.partial(place_kernel, n_pair, blocks),
        out_shape=[sds((rows, width)), sds((v_rows, width))],
        in_specs=[vmem] * 6,
        out_specs=[anywhere, anywhere],
        scratch_shapes=[held(rows, width), held(STEPS * width, width), held(width, width), dma((blocks + STEPS + 2,))],
        compiler_params=pltpu.CompilerParams(vmem_limit_bytes=8 * 1024 * 1024),
    )(turn, cs, *held_rows)


def solution(mesh):
    n_pair, n_row = mesh.shape["pair"], mesh.shape["row"]
    return jax.shard_map(
        functools.partial(body, n_pair, n_row),
        mesh=mesh,
        in_specs=(P("row", "pair"), P()),
        out_specs=(P("row", "pair"), P("row", "pair")),
        check_vma=False,
    )
```

```python
import functools

import jax
import jax.numpy as jnp
from jax import lax
from jax.experimental import pallas as pl
from jax.experimental.pallas import tpu as pltpu
from jax.sharding import PartitionSpec as P

B = 128
WIDTH = 2 * B
ROUNDS = 4
STEPS = 4
FETCHES = 4
EARLY = (7, 12, 12)
TILES = (2, 3, 3)
LATE = ((4, 6, 4, 4), (6, 2), (6, 2))
SETS = 14
ROWS_SENT = 4 * SETS
MESH = pl.DeviceIdType.MESH
F32 = jnp.float32

KEPT = [
    ([0, 1, 2, 3, 4], [5, 6, 7, 8, 9], [None, 10, 11, 12, 13]),
    ([0, 2], [1, 3], [None, 4]),
    ([0], [1], [None]),
]


def gram(x):
    return lax.dot_general(x, x, (((0,), (0,)), ((), ())), precision=lax.Precision.HIGHEST, preferred_element_type=F32)


def ahead(x, by):
    return pltpu.roll(x, lax.rem(B - by, B), 1)


def turns(offs_ref, step):
    offs = [offs_ref[step, r] for r in range(ROUNDS)]
    before = [jnp.int32(0)] + offs[:-1]
    return [lax.rem(b - o + B, B) for b, o in zip(before, offs)], offs[-1]


def distances(offs_ref, step):
    o = [offs_ref[step, r] for r in range(ROUNDS)]
    d1, d2, d3 = [lax.rem(b - a + B, B) for a, b in zip(o, o[1:])]
    near = [jnp.int32(0), d2, d3, d3 + d2, d3 - d2]
    far = near + [e + d1 for e in near] + [e - d1 for e in near[1:]]
    far = [lax.rem(e + 2 * B, B) for e in far]
    return o[0], (d1, d2, d3), [far, far[:5], [far[0], far[2]]]


def pick_diagonals(total, w_ref, dst_ref, offs_ref, step):
    o, _, far = distances(offs_ref, step)
    w_ref[0] = total[B:, B:]
    w_ref[1] = total[:B, B:]
    w_ref[2] = total[:B, :B]
    w_ref[3] = total[B:, :B]
    base = lax.broadcasted_iota(jnp.int32, (8, B), 0) - lax.broadcasted_iota(jnp.int32, (8, B), 1)
    same, to_first, to_second = far[0], [lax.rem(e - o + B, B) for e in far[0]], [lax.rem(e + o, B) for e in far[0]]
    for at, blocks in ((same, (0, 2)), (to_first, (1,)), (to_second, (3,))):
        acc = [[jnp.zeros((8, B), F32) for _ in at] for _ in blocks]
        for g in range(B // 8):
            dist = (base + 8 * g) & (B - 1)
            m = [w_ref[q, 8 * g : 8 * g + 8, :] for q in blocks]
            for i, t in enumerate(at):
                here = dist == t
                for n in range(len(blocks)):
                    acc[n][i] = jnp.where(here, m[n], acc[n][i])
        for n, q in enumerate(blocks):
            for i, v in enumerate(acc[n]):
                dst_ref[pl.ds(q * SETS + i, 1), :] = jnp.sum(v, axis=0, keepdims=True)
    dst_ref[pl.ds(0, 2 * SETS), :] = ahead(dst_ref[pl.ds(0, 2 * SETS), :], o)


def solve_angles(t_ref, offs_ref, step, cs_ref):
    _, turn, far = distances(offs_ref, step)
    d, e, a, b = [[t_ref[pl.ds(q * SETS + i, 1), :] for i in range(SETS)] for q in range(4)]
    for r in range(ROUNDS):
        gap = 0.5 * (d[0] - a[0])
        c0 = b[0]
        radius = jnp.sqrt(gap * gap + c0 * c0)
        sign = jnp.where(gap >= 0, 1.0, -1.0)
        t = -sign * c0 / (jnp.abs(gap) + radius + 1e-06 * (a[0] + d[0]))
        c = lax.rsqrt(1.0 + t * t)
        s = t * c
        cs_ref[pl.ds(r, 1), :] = c
        cs_ref[pl.ds(ROUNDS + r, 1), :] = s
        if r == ROUNDS - 1:
            break

        def partner(i):
            return (c, s) if i == 0 else (ahead(c, far[r][i]), ahead(s, far[r][i]))

        na, nb, nd, ne = [], [], [], []
        for i in KEPT[r][0]:
            cc, ss = partner(i)
            u1, u2 = cc * a[i] + ss * b[i], cc * e[i] + ss * d[i]
            v1, v2 = cc * b[i] - ss * a[i], cc * d[i] - ss * e[i]
            na.append(c * u1 + s * u2)
            nd.append(ahead(c * v2 - s * v1, turn[r]))
        for i in KEPT[r][1]:
            cc, ss = partner(i)
            v1, v2 = cc * b[i] - ss * a[i], cc * d[i] - ss * e[i]
            nb.append(c * v1 + s * v2)
        for i in KEPT[r][2]:
            if i is None:
                ne.append(nb[0])
                continue
            cc, ss = partner(i)
            u1, u2 = cc * a[i] + ss * b[i], cc * e[i] + ss * d[i]
            ne.append(ahead(c * u2 - s * u1, turn[r]))
        a, b, d, e = na, nb, nd, ne


def rotated(f, s, cs_ref, turn):
    shifts, back = turn
    for r in range(ROUNDS):
        s = pltpu.roll(s, shifts[r], 1)
        c = cs_ref[pl.ds(r, 1), :]
        n = cs_ref[pl.ds(ROUNDS + r, 1), :]
        f, s = f * c + s * n, s * c - f * n
    return f, pltpu.roll(s, back, 1)


def main_kernel(
    n_pair, n_row, rows, early, offs_hbm, x_hbm, x3f, x3s, w3f, w3s, cs_out, turn_out,
    offs_ref, x_in, xf, xs, of, os_, el, er, w_ref, gs, tot, cs, hl, hr, le, re,
    r0l, l0l, r0r, l0r, r1, l1, edge0, edge1,
    in_sem, g_send, g_recv, x_send, x_recv, e_send, e_recv, h_send, h_recv,
):
    k = lax.axis_index("pair")
    me = lax.axis_index("row")
    first, last = k == 0, k == n_pair - 1
    piece = rows // FETCHES
    late = []
    for n, sizes in zip(early, LATE):
        ends = [n + sum(sizes[: i + 1]) * (rows // 32) for i in range(len(sizes))]
        late.append([(end - size * (rows // 32), size * (rows // 32)) for end, size in zip(ends, sizes)])
    parts = [[(0, early[0])]] + [[(0, a)] + [(a, b - a)] * (b > a) for a, b in zip(early, early[1:])]

    fetch_offs = pltpu.make_async_copy(offs_hbm, offs_ref, in_sem.at[FETCHES])
    fetch_offs.start()
    fetch = [
        pltpu.make_async_copy(x_hbm.at[pl.ds(c * piece, piece)], x_in.at[pl.ds(c * piece, piece)], in_sem.at[c])
        for c in range(FETCHES)
    ]
    for copy in fetch:
        copy.start()

    barrier = pltpu.get_barrier_semaphore()

    @pl.when(k > 0)
    def _():
        pl.semaphore_signal(barrier, inc=1, device_id={"pair": k - 1}, device_id_type=MESH)

    @pl.when(k < n_pair - 1)
    def _():
        pl.semaphore_signal(barrier, inc=1, device_id={"pair": k + 1}, device_id_type=MESH)

    for j in range(1, n_row):
        pl.semaphore_signal(barrier, inc=1, device_id={"row": lax.rem(me + j, n_row)}, device_id_type=MESH)

    def to_right(src, dst, sems, at):
        return pltpu.make_async_remote_copy(
            src_ref=src, dst_ref=dst, send_sem=sems[0].at[(0,) + at], recv_sem=sems[1].at[(0,) + at],
            device_id={"pair": k + 1}, device_id_type=MESH,
        )

    def to_left(src, dst, sems, at):
        return pltpu.make_async_remote_copy(
            src_ref=src, dst_ref=dst, send_sem=sems[0].at[(1,) + at], recv_sem=sems[1].at[(1,) + at],
            device_id={"pair": k - 1}, device_id_type=MESH,
        )

    def arrived(dst_l, dst_r, sems, at):
        @pl.when(k > 0)
        def _():
            to_right(dst_l, dst_l, sems, at).wait_recv()

        @pl.when(k < n_pair - 1)
        def _():
            to_left(dst_r, dst_r, sems, at).wait_recv()

    def sent(src_r, src_l, sems, at):
        @pl.when(k < n_pair - 1)
        def _():
            to_right(src_r, src_r, sems, at).wait_send()

        @pl.when(k > 0)
        def _():
            to_left(src_l, src_l, sems, at).wait_send()

    def peer_copy(step, slot, to):
        return pltpu.make_async_remote_copy(
            src_ref=gs.at[step, slot], dst_ref=gs.at[step, slot], send_sem=g_send.at[step, to],
            recv_sem=g_recv.at[step, slot], device_id={"row": to}, device_id_type=MESH,
        )

    x_sems, e_sems, h_sems = (x_send, x_recv), (e_send, e_recv), (h_send, h_recv)

    def new(h, step):
        if step == STEPS - 2:
            return (x3f, x3s)[h]
        return (xf, xs)[h].at[step]

    def late_rows(step, c):
        return pl.ds(*late[step][c])

    def send_late(step, c):
        at = late_rows(step, c)
        f, s = of.at[step, at], os_.at[step, at]
        new_f, new_s = new(0, step).at[at], new(1, step).at[at]

        @pl.when(first)
        def _():
            to_right(s, new_f, x_sems, (step, c)).start()
            new_f[...] = f[...]

        @pl.when(jnp.logical_and(k > 0, k < n_pair - 1))
        def _():
            to_right(f, new_f, x_sems, (step, c)).start()

        @pl.when(last)
        def _():
            new_s[...] = f[...]

        @pl.when(k > 0)
        def _():
            to_left(s, new_s, x_sems, (step, c)).start()

    def early_moves(step, part):
        at = pl.ds(*parts[step][part])
        for h in range(2):
            if step == 0:
                src = x_in.at[at, pl.ds(h * B, B)]
                yield h, src, src, el.at[step, h, at], er.at[step, h, at]
            elif h == 0:
                yield h, new(0, step - 1).at[at], new(1, step - 1).at[at], el.at[step, 0, at], er.at[step, 1, at]

    def send_early(step, part):
        for h, to_r, to_l, from_l, from_r in early_moves(step, part):

            @pl.when(k < n_pair - 1)
            def _():
                to_right(to_r, from_l, e_sems, (step, h, part)).start()

            @pl.when(k > 0)
            def _():
                to_left(to_l, from_r, e_sems, (step, h, part)).start()

    def keep_own(step):
        top = pl.ds(0, early[step])
        own = [x_in.at[top, pl.ds(h * B, B)] if step == 0 else new(h, step - 1).at[top] for h in range(2)]

        @pl.when(first)
        def _():
            for h in range(2):
                el[step, h, top] = own[h][...]

        @pl.when(last)
        def _():
            for h in range(2):
                er[step, h, top] = own[h][...]

    def hold(step, at, f, s):
        el[step + 1, 1, at] = s
        er[step + 1, 0, at] = jnp.where(first, s, f)

    def rotate_own_early(step):
        top = pl.ds(0, early[step])
        if step == 0:
            f, s = x_in[top, :B], x_in[top, B:]
        else:
            f, s = xf[step - 1, top, :], xs[step - 1, top, :]
        f, s = rotated(f, s, cs.at[step], turns(offs_ref, step))
        hold(step, top, f, s)

    def early_gram(step):
        for part in range(len(parts[step])):
            for h, _, _, from_l, from_r in early_moves(step, part):
                arrived(from_l, from_r, e_sems, (step, h, part))
        turn = turns(offs_ref, step)
        tile = early[step] // TILES[step]
        total = jnp.zeros((WIDTH, WIDTH), F32)
        for c in range(TILES[step]):
            at = pl.ds(c * tile, tile)
            f, s = rotated(el[step, 0, at], el[step, 1, at], hl.at[step, step], turn)
            new_f = jnp.where(k == 1, s, f)
            f, s = rotated(er[step, 0, at], er[step, 1, at], hr.at[step, step], turn)
            new_s = jnp.where(last, f, s)
            new(0, step)[at, :] = new_f
            new(1, step)[at, :] = new_s
            total = total + gram(jnp.concatenate([new_f, new_s], axis=1))
        return total

    def send_history(step):
        if step > 0:
            le[step, pl.ds(0, step)] = hl[step - 1, pl.ds(0, step)]
            re[step, pl.ds(0, step)] = hr[step - 1, pl.ds(0, step)]
        le[step, step] = cs[step]
        re[step, step] = cs[step]
        n = pl.ds(0, step + 1)

        @pl.when(k < n_pair - 1)
        def _():
            to_right(le.at[step, n], hl.at[step, n], h_sems, (step,)).start()

        @pl.when(k > 0)
        def _():
            to_left(re.at[step, n], hr.at[step, n], h_sems, (step,)).start()

        @pl.when(first)
        def _():
            hl[step, n] = re[step, n]

        @pl.when(last)
        def _():
            hr[step, n] = le[step, n]

    def node(level, slot, cs_ref, from_left, from_right, dst_right, dst_left):
        turn = turns(offs_ref, level)
        outside = jnp.logical_or(slot < 0, slot >= n_pair)
        swap = jnp.logical_or(jnp.logical_or(slot < -1, slot == 0), slot >= n_pair)
        if level == 0:
            row = lax.broadcasted_iota(jnp.int32, (WIDTH, B), 0)
            col = lax.broadcasted_iota(jnp.int32, (WIDTH, B), 1)
            f, s = [jnp.where(row == col + h, 1.0, 0.0).astype(F32) for h in (0, B)]
        else:
            zero = jnp.zeros((WIDTH, B), F32)
            p = jnp.concatenate([from_left[...], zero], axis=0)
            q = jnp.concatenate([zero, from_right[...]], axis=0)
            f, s = jnp.where(outside, q, p), jnp.where(outside, p, q)
        f, s = rotated(f, s, cs_ref, turn)
        if dst_right is not None:
            dst_right[...] = jnp.where(swap, s, f)
        if dst_left is not None:
            dst_left[...] = jnp.where(swap, f, s)

    def rebuild(step):
        if step == 1:
            node(0, k - 1, hl.at[0, 0], None, None, r0l, l0l)
            node(0, k + 1, hr.at[0, 0], None, None, r0r, l0r)
        if step == 2:
            node(1, k, cs.at[1], r0l, l0r, r1, l1)
        if step == 3:
            node(0, k - 3, hl.at[2, 0], None, None, edge0.at[0], None)
            node(0, k + 3, hr.at[2, 0], None, None, None, edge0.at[1])
            node(1, k - 2, hl.at[2, 1], edge0.at[0], l0l, edge1.at[0], None)
            node(1, k + 2, hr.at[2, 1], r0r, edge0.at[1], None, edge1.at[1])
            node(2, k - 1, hl.at[2, 2], edge1.at[0], l1, w3f, None)
            node(2, k + 1, hr.at[2, 2], r1, edge1.at[1], None, w3s)

    total = jnp.zeros((WIDTH, WIDTH), F32)
    for c in range(FETCHES // 2):
        fetch[c].wait()
        total = total + gram(x_in[pl.ds(c * piece, piece), :])
    pl.semaphore_wait(barrier, n_row - 1 + (k > 0).astype(jnp.int32) + (k < n_pair - 1).astype(jnp.int32))
    send_early(0, 0)
    keep_own(0)
    for c in range(FETCHES // 2, FETCHES):
        fetch[c].wait()
        total = total + gram(x_in[pl.ds(c * piece, piece), :])
    fetch_offs.wait()
    for step in range(STEPS):
        pick_diagonals(total, w_ref, gs.at[step, me], offs_ref, step)
        for j in sorted(range(1, n_row), key=lambda j: -min(j, n_row - j)):
            peer_copy(step, me, lax.rem(me + j, n_row)).start()
        if 0 < step < STEPS - 1:
            rotate_own_early(step - 1)
            keep_own(step)
        rebuild(step)
        for j in range(1, n_row):
            peer_copy(step, lax.rem(me + j, n_row), lax.rem(me + j, n_row)).wait_recv()
        tot[...] = sum((gs[step, i] for i in range(1, n_row)), gs[step, 0])
        solve_angles(tot, offs_ref, step, cs.at[step])
        if step == STEPS - 1:
            break
        turn = turns(offs_ref, step)
        send_history(step)
        for c in range(len(late[step])):
            at = late_rows(step, c)
            if step == 0:
                f, s = x_in[at, :B], x_in[at, B:]
            else:
                f, s = xf[step - 1, at, :], xs[step - 1, at, :]
            f, s = rotated(f, s, cs.at[step], turn)
            of[step, at, :] = f
            os_[step, at, :] = s
            send_late(step, c)
            if step + 1 < STEPS - 1 and sum(late[step][c]) <= early[step + 1]:
                hold(step, at, f, s)
        n = pl.ds(0, step + 1)
        arrived(hl.at[step, n], hr.at[step, n], h_sems, (step,))
        total = early_gram(step)
        if step + 1 < STEPS - 1:
            send_early(step + 1, 0)
        for c in range(len(late[step])):
            at = late_rows(step, c)
            arrived(new(0, step).at[at], new(1, step).at[at], x_sems, (step, c))
            if step + 1 < STEPS - 1 and len(parts[step + 1]) > 1 and sum(late[step][c]) == early[step + 1]:
                send_early(step + 1, 1)
            total = total + gram(jnp.concatenate([new(h, step)[at, :] for h in range(2)], axis=1))

    cs_out[...] = cs[STEPS - 1]
    shifts, back = turns(offs_ref, STEPS - 1)
    row = lax.broadcasted_iota(jnp.int32, (2 * ROUNDS, B), 0)
    table = jnp.full((2 * ROUNDS, B), back, jnp.int32)
    for r in range(ROUNDS):
        table = jnp.where(row == r, shifts[r], table)
    turn_out[...] = table

    for step in range(STEPS):
        for j in range(1, n_row):
            peer_copy(step, me, lax.rem(me + j, n_row)).wait_send()
        if step < STEPS - 1:
            n = pl.ds(0, step + 1)
            sent(le.at[step, n], re.at[step, n], h_sems, (step,))
            for part in range(len(parts[step])):
                for h, to_r, to_l, _, _ in early_moves(step, part):
                    sent(to_r, to_l, e_sems, (step, h, part))
            for c in range(len(late[step])):
                at = late_rows(step, c)
                sent(of.at[step, at], os_.at[step, at], x_sems, (step, c))


def place_kernel(n_pair, blocks, turn_ref, cs_ref, xf, xs, wf, ws, x_out, v_out, x_last, w_last, zero, sem):
    k, me = lax.axis_index("pair"), lax.axis_index("row")
    half = xf.shape[0] // 2
    zero[...] = jnp.zeros_like(zero)
    slots = []
    for j in range(STEPS):
        slot = k - (STEPS - 1) + 2 * j
        slot = jnp.where(slot < 0, -1 - slot, slot)
        slots.append(jnp.where(slot >= n_pair, 2 * n_pair - 1 - slot, slot) - me * blocks)

    def piece(j):
        here = jnp.logical_and(slots[j] >= 0, slots[j] < blocks)
        place = pl.multiple_of(jnp.where(here, slots[j], 0) * WIDTH, WIDTH)
        return here, pltpu.make_async_copy(
            w_last.at[pl.ds(j * WIDTH, WIDTH)], v_out.at[pl.ds(place, WIDTH)], sem.at[blocks + j]
        )

    def blank(b):
        empty = slots[0] != b
        for j in range(1, STEPS):
            empty = jnp.logical_and(empty, slots[j] != b)
        return empty, pltpu.make_async_copy(zero, v_out.at[pl.ds(b * WIDTH, WIDTH)], sem.at[b])

    pieces, blanks = [piece(j) for j in range(STEPS)], [blank(b) for b in range(blocks)]
    for needed, copy in blanks:
        pl.when(needed)(copy.start)
    turn = [turn_ref[r, 0] for r in range(ROUNDS)], turn_ref[ROUNDS, 0]
    moves = []
    for g in range(2):
        at = pl.ds(g * half, half)
        f, s = rotated(xf[at, :], xs[at, :], cs_ref, turn)
        x_last[at, :B] = f
        x_last[at, B:] = s
        moves.append(pltpu.make_async_copy(x_last.at[at], x_out.at[at], sem.at[blocks + STEPS + g]))
        moves[-1].start()
    blank_rows = jnp.zeros((WIDTH, B), F32)
    parts = [
        (wf[: 2 * WIDTH, :], jnp.concatenate([blank_rows, ws[:WIDTH, :]], axis=0)),
        (jnp.concatenate([wf[2 * WIDTH :, :], blank_rows], axis=0), ws[WIDTH:, :]),
    ]
    for g, (f, s) in enumerate(parts):
        at = pl.ds(g * 2 * WIDTH, 2 * WIDTH)
        f, s = rotated(f, s, cs_ref, turn)
        w_last[at, :B] = f
        w_last[at, B:] = s
        for needed, copy in pieces[2 * g : 2 * g + 2]:
            pl.when(needed)(copy.start)
    for needed, copy in pieces + blanks:
        pl.when(needed)(copy.wait)
    for copy in moves:
        copy.wait()


def body(n_pair, n_row, whitened, offsets):
    rows, width = whitened.shape
    v_rows = n_pair * width // n_row
    blocks = v_rows // width
    early = [rows * n // 16 for n in EARLY]
    sds = functools.partial(jax.ShapeDtypeStruct, dtype=F32)
    vmem = pl.BlockSpec(memory_space=pltpu.VMEM)
    anywhere = pl.BlockSpec(memory_space=pl.ANY)
    hbm = pl.BlockSpec(memory_space=pltpu.HBM)
    dma = pltpu.SemaphoreType.DMA

    def held(*shape):
        return pltpu.VMEM(shape, F32)

    *held_rows, cs, turn = pl.pallas_call(
        functools.partial(main_kernel, n_pair, n_row, rows, early),
        out_shape=[sds((rows, B))] * 2
        + [sds(((STEPS - 1) * width, B))] * 2
        + [sds((2 * ROUNDS, B)), jax.ShapeDtypeStruct((2 * ROUNDS, B), jnp.int32)],
        in_specs=[hbm, hbm],
        out_specs=[vmem] * 6,
        scratch_shapes=[
            pltpu.SMEM((STEPS, ROUNDS), jnp.int32),
            held(rows, width),
            held(STEPS - 2, rows, B),
            held(STEPS - 2, rows, B),
            held(STEPS - 1, rows, B),
            held(STEPS - 1, rows, B),
            held(STEPS - 1, 2, max(early), B),
            held(STEPS - 1, 2, max(early), B),
            held(4, B, B),
            held(STEPS, n_row, ROWS_SENT, B),
            held(ROWS_SENT, B),
            held(STEPS, 2 * ROUNDS, B),
        ]
        + [held(STEPS - 1, STEPS - 1, 2 * ROUNDS, B) for _ in range(4)]
        + [held(n * width, B) for n in (1, 1, 1, 1, 2, 2)]
        + [held(2, width, B), held(2, 2 * width, B)]
        + [
            dma((FETCHES + 1,)),
            dma((STEPS, n_row)),
            dma((STEPS, n_row)),
            dma((2, STEPS - 1, max(map(len, LATE)))),
            dma((2, STEPS - 1, max(map(len, LATE)))),
            dma((2, STEPS - 1, 2, 2)),
            dma((2, STEPS - 1, 2, 2)),
            dma((2, STEPS - 1)),
            dma((2, STEPS - 1)),
        ],
        compiler_params=pltpu.CompilerParams(
            collective_id=0, has_side_effects=True, vmem_limit_bytes=40 * 1024 * 1024
        ),
    )(pltpu.with_memory_space_constraint(offsets, pltpu.HBM), pltpu.with_memory_space_constraint(whitened, pltpu.HBM))
    return pl.pallas_call(
        functools.partial(place_kernel, n_pair, blocks),
        out_shape=[sds((rows, width)), sds((v_rows, width))],
        in_specs=[vmem] * 6,
        out_specs=[anywhere, anywhere],
        scratch_shapes=[held(rows, width), held(STEPS * width, width), held(width, width), dma((blocks + STEPS + 2,))],
        compiler_params=pltpu.CompilerParams(vmem_limit_bytes=8 * 1024 * 1024),
    )(turn, cs, *held_rows)


def solution(mesh):
    n_pair, n_row = mesh.shape["pair"], mesh.shape["row"]
    return jax.shard_map(
        functools.partial(body, n_pair, n_row),
        mesh=mesh,
        in_specs=(P("row", "pair"), P()),
        out_specs=(P("row", "pair"), P("row", "pair")),
        check_vma=False,
    )
```
